32 devices in a mesh: mom: 2 (over x), pts: 16 (over z, y, core).
Axes of the slice: x: 2, y: 2, z: 4, core: 2. Of those that a mesh axis runs over, the one named last changes fastest.
Arguments:
- amplitudes: bfloat16 [2, 2, 1, 256, 64, 128], P(None, None, None, 'mom'), may hold values from -6 to 6
- val_orbitals: bfloat16 [2, 256, 64, 512], P(None, 'mom'), may hold values from -0.25 to 0.25
- cond_orbitals: bfloat16 [2, 256, 512, 128], P(None, 'mom', 'pts'), may hold values from -0.25 to 0.25
- screened: bfloat16 [2, 256, 512, 512], P(None, None, ('pts', 'mom')), may hold values from -12 to 12
- val_energy: float32 [256, 64], P('mom', 'pts'), may hold values from -2 to -0.5
- cond_energy: float32 [256, 128], P('mom'), may hold values from 0.5 to 2
- grid_of_slot: int32 [256], replicated, may hold values from 0 to 255, as said below
- opposite_slot: int32 [256], P('mom'), may hold values from 0 to 255, as said below
Outputs:
- applied: float32 [2, 2, 1, 256, 64, 128], P(None, None, None, 'mom', 'pts')
The draws below stay inside these ranges and needn't reach their ends.
Inputs may be any that keep to these rules, and one draw needn't show every extreme that they name: `grid_of_slot`: a permutation of the grid indices. opposite_slot[s] is the slot whose grid index is 255 - grid_of_slot[s]; it is never s, and s and opposite_slot[s] lie in aligned blocks of 128 slots whose first slots differ by 128.
All inputs are finite; a program needn't handle non-finite values.
Results may differ from the reference program's by a relative error of at most 0.006.
Values may be sent and summed in bfloat16 or wider, within the bound.
No kernel may reach another device: no remote copies, remote signals or barrier semaphores. Data moves between devices by JAX's collectives and lax.ppermute only.
A program may use at most 256 MiB of HBM per device.

```python
import math
import jax
import jax.numpy as jnp
from jax import lax

NV = 64
NC = 128
NP = 512
NK = 256
NVEC = 1
KD = 128


def pairing(key):
    half_count = NK // 2
    blocks = half_count // KD
    base_key = jax.random.fold_in(key, 11)
    key_perm, key_flip, key_order = jax.random.split(base_key, 3)
    lower_grid = jax.random.permutation(key_perm, half_count).astype(jnp.int32)
    flip_bits = jax.random.randint(key_flip, (half_count,), 0, 2)
    lower_grid = jnp.where(flip_bits == 1, NK - 1 - lower_grid, lower_grid)
    scores = jax.random.randint(key_order, (blocks, KD), 0, 1 << 20) * KD + jnp.arange(KD, dtype=jnp.int32)[None, :]
    within = jnp.argsort(scores, axis=1, stable=True).astype(jnp.int32)
    partner_low = (jnp.arange(blocks, dtype=jnp.int32)[:, None] * KD + within).reshape(half_count)
    upper_grid = NK - 1 - lower_grid[partner_low]
    grid_index = jnp.concatenate([lower_grid, upper_grid]).astype(jnp.int32)
    upper_slots = half_count + jnp.arange(half_count, dtype=jnp.int32)
    opposite = jnp.zeros((NK,), jnp.int32).at[upper_slots].set(partner_low).at[partner_low].set(upper_slots)
    return (grid_index, opposite)


def draw_grid_of_slot(key, part):
    return pairing(key)[0]


def draw_opposite_slot(key, part):
    return pairing(key)[1]


def levels(rng, extent, shards, least, top_value):
    def one(position, blocks):
        draws = jax.random.uniform(jax.random.fold_in(jax.random.fold_in(rng, 6), position), (blocks,), jnp.float32, least / len(shards), top_value / len(shards))
        return jnp.repeat(jnp.exp(draws), extent[position] // blocks).reshape((-1,) + (1,) * (len(extent) - position - 1))

    gain = one(*shards[0])
    for cut in shards[1:]:
        gain = gain * one(*cut)
    return gain


def noise(stream_key, dims, width, reach, cuts=(), kind=jnp.bfloat16):
    drawn = width * jax.random.normal(stream_key, dims, jnp.float32)
    if cuts:
        drawn = drawn * levels(stream_key, dims, cuts, -0.22, 0.18)
    return jnp.clip(drawn, -reach, reach).astype(kind)


def setup_inputs(seed: int = 0) -> dict:
    key_list = jax.random.split(jax.random.key(seed), 9)
    return {
        "amplitudes": noise(key_list[0], (2, 2, NVEC, NK, NV, NC), 1.0, 6.0, ((3, 2),)),
        "val_orbitals": noise(key_list[1], (2, NK, NV, NP), NP ** -0.5, 0.25, ((1, 2),)),
        "cond_orbitals": noise(key_list[2], (2, NK, NP, NC), NP ** -0.5, 0.25, ((1, 2), (2, 16))),
        "screened": noise(key_list[3], (2, NK, NP, NP), 2.0, 12.0, ((2, 32),)),
        "val_energy": jnp.clip(-2.0 + 1.5 * jax.random.uniform(key_list[4], (NK, NV), jnp.float32) ** levels(key_list[4], (NK, NV), ((0, 2), (1, 16)), -0.2, 0.2), -2.0, -0.5),
        "cond_energy": jnp.clip(0.5 + 1.5 * jax.random.uniform(key_list[5], (NK, NC), jnp.float32) ** levels(key_list[5], (NK, NC), ((0, 2),), -0.2, 0.2), 0.5, 2.0),
        "grid_of_slot": draw_grid_of_slot(jax.random.fold_in(key_list[8], 71), 0),
        "opposite_slot": draw_opposite_slot(jax.random.fold_in(key_list[8], 71), 0),
    }


def complex_mix(formula, left, right, left_sign, right_sign):
    left_real = left[0].astype(jnp.float32)
    left_imag = left[1].astype(jnp.float32)
    right_real = right[0].astype(jnp.float32)
    right_imag = right[1].astype(jnp.float32)
    high = lax.Precision.HIGHEST
    real_real = jnp.einsum(formula, left_real, right_real, precision=high)
    imag_imag = jnp.einsum(formula, left_imag, right_imag, precision=high)
    real_imag = jnp.einsum(formula, left_real, right_imag, precision=high)
    imag_real = jnp.einsum(formula, left_imag, right_real, precision=high)
    return jnp.stack([real_real - left_sign * right_sign * imag_imag,
                      right_sign * real_imag + left_sign * imag_real])


def reference(amplitudes, val_orbitals, cond_orbitals, screened, val_energy, cond_energy, grid_of_slot, opposite_slot):
    frequency = jnp.arange(NK, dtype=jnp.int32)
    phases = (frequency[:, None] * grid_of_slot[None, :]) % NK
    angles = phases.astype(jnp.float32) * (2.0 * math.pi / NK)
    cosine_table = jnp.cos(angles).astype(jnp.bfloat16)
    sine_table = jnp.sin(angles).astype(jnp.bfloat16)
    nu_block = NP // 8
    fields = jnp.swapaxes(amplitudes.reshape(2, 2 * NVEC, NK, NV, NC), 0, 1)

    def one_field(coefficient):
        def accumulate(running, offset):
            cond_block = lax.dynamic_slice_in_dim(cond_orbitals, offset, nu_block, 2)
            screen_block = lax.dynamic_slice_in_dim(screened, offset, nu_block, 2)
            half_product = complex_mix("kvc,kuc->kvu", coefficient, cond_block, 1.0, 1.0).astype(jnp.bfloat16)
            pair_values = complex_mix("kvu,kvm->kum", half_product, val_orbitals, 1.0, -1.0).astype(jnp.bfloat16)
            flattened = pair_values.reshape(2, NK, nu_block * NP)
            spec_real = (jnp.dot(cosine_table, flattened[0], preferred_element_type=jnp.float32)
                         + jnp.dot(sine_table, flattened[1], preferred_element_type=jnp.float32))
            spec_imag = (jnp.dot(cosine_table, flattened[1], preferred_element_type=jnp.float32)
                         - jnp.dot(sine_table, flattened[0], preferred_element_type=jnp.float32))
            screen_flat = screen_block.reshape(2, NK, nu_block * NP).astype(jnp.float32)
            prod_real = (screen_flat[0] * spec_real - screen_flat[1] * spec_imag).astype(jnp.bfloat16)
            prod_imag = (screen_flat[0] * spec_imag + screen_flat[1] * spec_real).astype(jnp.bfloat16)
            back_real = (jnp.dot(cosine_table.T, prod_real, preferred_element_type=jnp.float32)
                         - jnp.dot(sine_table.T, prod_imag, preferred_element_type=jnp.float32)) * (1.0 / NK)
            back_imag = (jnp.dot(cosine_table.T, prod_imag, preferred_element_type=jnp.float32)
                         + jnp.dot(sine_table.T, prod_real, preferred_element_type=jnp.float32)) * (1.0 / NK)
            field_pts = jnp.stack([back_real, back_imag]).astype(jnp.bfloat16).reshape(2, NK, nu_block, NP)
            weighted = complex_mix("kum,kvm->kvu", field_pts, val_orbitals, 1.0, 1.0).astype(jnp.bfloat16)
            return running + complex_mix("kvu,kuc->kvc", weighted, cond_block, 1.0, -1.0), None

        offsets = jnp.arange(8, dtype=jnp.int32) * nu_block
        start_sum = jnp.zeros((2, NK, NV, NC), jnp.float32)
        result_sum, unused = lax.scan(accumulate, start_sum, offsets)
        return result_sum

    band_values = lax.map(one_field, fields)
    band_values = jnp.swapaxes(band_values, 0, 1).reshape(2, 2, NVEC, NK, NV, NC)
    mirrored = jnp.take(band_values, opposite_slot, axis=3)
    energy_gap = cond_energy[:, None, :] - val_energy[:, :, None]
    own_rows = amplitudes.astype(jnp.float32)
    result_real = energy_gap * own_rows[0, 0] - band_values[0, 0] - mirrored[0, 1]
    result_imag = energy_gap * own_rows[1, 0] - band_values[1, 0] + mirrored[1, 1]
    anti_real = -energy_gap * own_rows[0, 1] + band_values[0, 1] + mirrored[0, 0]
    anti_imag = -energy_gap * own_rows[1, 1] + band_values[1, 1] - mirrored[1, 0]
    return jnp.stack([jnp.stack([result_real, anti_real]), jnp.stack([result_imag, anti_imag])])
```

```python
import functools
import math

import jax
import jax.numpy as jnp
from jax import lax
from jax.experimental import pallas as pl
from jax.experimental.pallas import tpu as pltpu
from jax.sharding import PartitionSpec as P

F32 = jnp.float32
BF16 = jnp.bfloat16
MIB = 1024 * 1024


def partner_2(value, axis, apart):
    mask = 2**apart
    pairs = [(source, source ^ mask) for source in range(lax.axis_size(axis))]
    return lax.ppermute(value, axis, pairs)


def complex_mix(formula, left, right, left_sign, right_sign):
    real_real = jnp.einsum(formula, left[0], right[0], preferred_element_type=jnp.float32)
    imag_imag = jnp.einsum(formula, left[1], right[1], preferred_element_type=jnp.float32)
    real_imag = jnp.einsum(formula, left[0], right[1], preferred_element_type=jnp.float32)
    imag_real = jnp.einsum(formula, left[1], right[0], preferred_element_type=jnp.float32)
    return jnp.stack(
        [
            real_real - left_sign * right_sign * imag_imag,
            right_sign * real_imag + left_sign * imag_real,
        ]
    )


def general_path(
    amplitudes,
    val_orbitals,
    cond_orbitals,
    screened,
    val_energy,
    cond_energy,
    grid_of_slot,
    opposite_slot,
):
    slots_here = opposite_slot.shape[0]
    total_slots = grid_of_slot.shape[0]
    rows_here = val_energy.shape[1]
    frequency = jnp.arange(total_slots, dtype=jnp.int32)
    phases = frequency[:, None] * grid_of_slot[None, :] % total_slots
    angles = phases.astype(jnp.float32) * (2.0 * math.pi / total_slots)
    cosine_table = jnp.cos(angles).astype(jnp.bfloat16)
    sine_table = jnp.sin(angles).astype(jnp.bfloat16)
    half_product = complex_mix("bnkvc,kuc->bnkvu", amplitudes, cond_orbitals, 1.0, 1.0).astype(
        jnp.bfloat16
    )
    pair_values = complex_mix("bnkvu,kvm->bnkum", half_product, val_orbitals, 1.0, -1.0).astype(
        jnp.bfloat16
    )
    flattened = pair_values.reshape(pair_values.shape[:4] + (-1,))
    weights = screened.reshape(2, total_slots, -1)
    inverse_count = 1.0 / total_slots
    whole_k = lax.all_to_all(flattened, "mom", split_axis=4, concat_axis=3, tiled=True)
    spec_real = jnp.einsum(
        "fs,bnsc->bnfc", cosine_table, whole_k[0], preferred_element_type=jnp.float32
    ) + jnp.einsum("fs,bnsc->bnfc", sine_table, whole_k[1], preferred_element_type=jnp.float32)
    spec_imag = jnp.einsum(
        "fs,bnsc->bnfc", cosine_table, whole_k[1], preferred_element_type=jnp.float32
    ) - jnp.einsum("fs,bnsc->bnfc", sine_table, whole_k[0], preferred_element_type=jnp.float32)
    prod_real = (weights[0] * spec_real - weights[1] * spec_imag).astype(jnp.bfloat16)
    prod_imag = (weights[0] * spec_imag + weights[1] * spec_real).astype(jnp.bfloat16)
    back_real = (
        jnp.einsum("fs,bnfc->bnsc", cosine_table, prod_real, preferred_element_type=jnp.float32)
        - jnp.einsum("fs,bnfc->bnsc", sine_table, prod_imag, preferred_element_type=jnp.float32)
    ) * inverse_count
    back_imag = (
        jnp.einsum("fs,bnfc->bnsc", cosine_table, prod_imag, preferred_element_type=jnp.float32)
        + jnp.einsum("fs,bnfc->bnsc", sine_table, prod_real, preferred_element_type=jnp.float32)
    ) * inverse_count
    field_pts = lax.all_to_all(
        jnp.stack([back_real, back_imag]).astype(jnp.bfloat16),
        "mom",
        split_axis=3,
        concat_axis=4,
        tiled=True,
    )
    field_pts = field_pts.reshape(pair_values.shape)
    weighted = complex_mix("bnkum,kvm->bnkvu", field_pts, val_orbitals, 1.0, 1.0).astype(
        jnp.bfloat16
    )
    rows_mine = lax.all_to_all(weighted, "pts", split_axis=4, concat_axis=5, tiled=True)
    band_values = complex_mix(
        "bnkvu,kuc->bnkvc",
        rows_mine,
        lax.all_gather(cond_orbitals, "pts", axis=2, tiled=True),
        1.0,
        -1.0,
    )
    top_bit = lax.axis_size("mom").bit_length() - 2
    partner = partner_2(band_values.astype(jnp.bfloat16), "mom", top_bit).astype(band_values.dtype)
    mirrored = jnp.take(partner, opposite_slot % slots_here, axis=3)
    start_row = lax.axis_index("pts") * rows_here
    own_rows = lax.dynamic_slice_in_dim(amplitudes, start_row, rows_here, 4).astype(jnp.float32)
    energy_gap = cond_energy[:, None, :] - val_energy[:, :, None]
    result_real = energy_gap * own_rows[0, 0] - band_values[0, 0] - mirrored[0, 1]
    result_imag = energy_gap * own_rows[1, 0] - band_values[1, 0] + mirrored[1, 1]
    anti_real = -energy_gap * own_rows[0, 1] + band_values[0, 1] + mirrored[0, 0]
    anti_imag = -energy_gap * own_rows[1, 1] + band_values[1, 1] - mirrored[1, 0]
    return jnp.stack([jnp.stack([result_real, anti_real]), jnp.stack([result_imag, anti_imag])])


def half_signs(low, high):
    lane = lax.broadcasted_iota(jnp.int32, (1, 128), 1)
    return jnp.where(lane < 64, low, high).astype(F32)


def half_body(where_ref, amp_ref, cond_ref, out_ref):
    groups, block, _, points, _ = out_ref.shape
    total = groups * points
    signs = half_signs(-1.0, 1.0)
    for kk in range(block):
        cond = cond_ref[:, kk].reshape(2 * total, cond_ref.shape[-1])
        for b in range(2):
            amp = amp_ref[:, b, 0, kk].reshape(128, amp_ref.shape[-1])
            full = lax.dot_general(
                cond, amp, (((1,), (1,)), ((), ())), preferred_element_type=F32
            )
            half = full[:total] + pltpu.roll(full[total:], 64, 1) * signs
            half = half.astype(BF16).reshape(groups, points, 128)
            for g in range(groups):
                out_ref[where_ref[g], kk, b] = half[g]


def half_call(amplitudes, cond_orbitals, where, groups):
    slots, bands = amplitudes.shape[3], amplitudes.shape[5]
    rows = amplitudes.shape[4]
    points = cond_orbitals.shape[2] // groups
    block = 16
    return pl.pallas_call(
        half_body,
        out_shape=jax.ShapeDtypeStruct((groups, slots, 2, points, 128), BF16),
        grid_spec=pltpu.PrefetchScalarGridSpec(
            num_scalar_prefetch=1,
            grid=(slots // block,),
            in_specs=[
                pl.BlockSpec((2, 2, 1, block, rows, bands), lambda i, *_: (0, 0, 0, i, 0, 0)),
                pl.BlockSpec((2, block, groups * points, bands), lambda i, *_: (0, i, 0, 0)),
            ],
            out_specs=pl.BlockSpec(
                (groups, block, 2, points, 128), lambda i, *_: (0, i, 0, 0, 0)
            ),
        ),
        compiler_params=pltpu.CompilerParams(vmem_limit_bytes=40 * MIB),
    )(where, amplitudes, cond_orbitals)


def main_body(layout, base_ref, pos_ref, *refs):
    own_blocks, block, sizes, points, first, last = layout
    half_own, half_other, own_ref = refs[:3]
    count = sum(len(group) for group in sizes)
    flat = list(refs[3 : 3 + count])
    groups = []
    for group in sizes:
        groups.append([flat.pop(0) for _ in group])
    rest = list(refs[3 + count :])
    screen_ref, forward_ref, backward_ref = rest[:3]
    rest = rest[3:]
    before_ref = None if first else rest.pop(0)
    out_ref, pair_ref = rest
    blocks = own_blocks + len(groups)
    total = blocks * block
    rows = 4 * points
    lanes = pair_ref.shape[0]
    width = lanes * 128
    step = pl.program_id(0)
    into = half_signs(1.0, -1.0)
    back = half_signs(-1.0, 1.0)

    def make_pairs(source, half_ref, half_start, start, size):
        for kk in range(size):
            half = half_ref[half_start + kk].reshape(2 * points, 128)
            turned = (pltpu.roll(half.astype(F32), 64, 1) * into).astype(BF16)
            stacked = jnp.concatenate([half, turned], axis=0)
            val = source[:, kk].reshape(128, width)
            pairs = jnp.dot(stacked, val, preferred_element_type=F32)
            at = pl.multiple_of((start + kk) * rows, rows)
            for l in range(lanes):
                pair_ref[l, pl.ds(at, rows), :] = pairs[:, l * 128 : (l + 1) * 128]

    def make_weighted(source, half_ref, half_start, start, size):
        for kk in range(size):
            k = start + kk
            at = pl.multiple_of(k * rows, rows)
            field = jnp.concatenate(
                [pair_ref[l, pl.ds(at, rows), :] for l in range(lanes)], axis=1
            ).astype(BF16)
            val = source[:, kk].reshape(128, width)
            both = lax.dot_general(
                field, val, (((1,), (1,)), ((), ())), preferred_element_type=F32
            )
            half = rows // 2
            weighted = both[:half] + pltpu.roll(both[half:], 64, 1) * back
            if not first:
                weighted = before_ref[k] + weighted
            if last:
                out_ref[pos_ref[k]] = weighted.astype(BF16).reshape(2, points, 128)
            else:
                out_ref[k] = weighted

    def each_block(work, index):
        @pl.when(index < own_blocks)
        def _():
            work(own_ref, half_own, index * block, index * block, block)

        for t, (group, extents) in enumerate(zip(groups, sizes)):

            @pl.when(index == own_blocks + t)
            def _():
                done = 0
                for ref, extent in zip(group, extents):
                    start = (own_blocks + t) * block + done
                    work(ref, half_other, base_ref[t] + done, start, extent)
                    done += extent

    @pl.when(step < blocks)
    def _():
        each_block(make_pairs, step)

    @pl.when((step >= blocks) & (step < blocks + points))
    def _():
        nu = step - blocks
        for l in range(lanes):
            columns = []
            for b in range(2):
                parts = []
                for ri in range(2):
                    row = ri * 2 * points + b * points + nu
                    parts.append(pair_ref[l, pl.ds(row, total, stride=rows), :].astype(BF16))
                columns.append(jnp.concatenate(parts, axis=0))
            spectrum = jnp.dot(
                forward_ref[...], jnp.concatenate(columns, axis=1), preferred_element_type=F32
            )
            real = screen_ref[0, 0, :, l * 128 : (l + 1) * 128].astype(F32)
            imag = screen_ref[0, 1, :, l * 128 : (l + 1) * 128].astype(F32)
            real = jnp.concatenate([real, real], axis=1)
            imag = jnp.concatenate([imag, imag], axis=1)
            spec_real, spec_imag = spectrum[:total], spectrum[total:]
            prod_real = (real * spec_real - imag * spec_imag).astype(BF16)
            prod_imag = (real * spec_imag + imag * spec_real).astype(BF16)
            field = jnp.dot(
                backward_ref[...],
                jnp.concatenate([prod_real, prod_imag], axis=0),
                preferred_element_type=F32,
            )
            for b in range(2):
                for ri in range(2):
                    row = ri * 2 * points + b * points + nu
                    pair_ref[l, pl.ds(row, total, stride=rows), :] = field[
                        ri * total : (ri + 1) * total, b * 128 : (b + 1) * 128
                    ]

    @pl.when(step >= blocks + points)
    def _():
        each_block(make_weighted, step - blocks - points)


def main_call(half_own, half_other, own, chunk, pieces, screen, tables, base, pos, before, last):
    slots, _, points, _ = half_own.shape
    bands = own.shape[2]
    block = sum(piece.shape[1] for piece in pieces[0])
    width = pieces[0][0].shape[3]
    own_blocks = slots // block
    blocks = own_blocks + len(pieces)
    total = blocks * block
    first = before is None
    sizes = tuple(tuple(piece.shape[1] for piece in group) for group in pieces)
    flat = [piece for group in pieces for piece in group]

    def own_map(s, *_):
        early = jnp.minimum(s, own_blocks - 1)
        late = jnp.clip(s - blocks - points, 0, own_blocks - 1)
        return (0, jnp.where(s < blocks, early, late), 0, chunk)

    def whole(shape):
        return pl.BlockSpec(
            shape, lambda s, *_: (0,) * len(shape), pipeline_mode=pl.Buffered(1)
        )

    in_specs = [
        whole(half_own.shape),
        whole(half_other.shape),
        pl.BlockSpec((2, block, bands, width), own_map),
    ]
    in_specs += [whole(piece.shape) for piece in flat]
    in_specs += [
        pl.BlockSpec(
            (1, 2, total, width), lambda s, *_: (jnp.clip(s - blocks, 0, points - 1), 0, 0, chunk)
        ),
        whole(tables[0].shape),
        whole(tables[1].shape),
    ]
    operands = [half_own, half_other, own, *flat, screen, *tables]
    if not first:
        in_specs.append(whole(before.shape))
        operands.append(before)
    if last:
        out = jax.ShapeDtypeStruct((total, 2, points, 128), BF16)
    else:
        out = jax.ShapeDtypeStruct((total, 2 * points, 128), F32)
    return pl.pallas_call(
        functools.partial(main_body, (own_blocks, block, sizes, points, first, last)),
        out_shape=out,
        grid_spec=pltpu.PrefetchScalarGridSpec(
            num_scalar_prefetch=2,
            grid=(2 * blocks + points,),
            in_specs=in_specs,
            out_specs=whole(out.shape),
            scratch_shapes=[pltpu.VMEM((width // 128, total * 4 * points, 128), F32)],
        ),
        compiler_params=pltpu.CompilerParams(vmem_limit_bytes=60 * MIB),
    )(base, pos, *operands)


def final_body(weighted_ref, cond_ref, out_ref, lay_ref):
    sources = weighted_ref.shape[0]
    points = weighted_ref.shape[4]
    holders = cond_ref.shape[1]
    groups = sources // holders
    sums = {}
    for h in range(2):
        columns = []
        for ri in range(2):
            parts = []
            for g in range(groups):
                part = cond_ref[h, :, 0, ri, g * points : (g + 1) * points, :]
                parts.append(part.reshape(holders * points, 128))
            columns.append(jnp.concatenate(parts, axis=0))
        cond = jnp.concatenate(columns, axis=1)
        for b in range(2):
            weighted = weighted_ref[:, h, 0, b].reshape(sources * points, 128)
            full = lax.dot_general(
                weighted, cond, (((0,), (0,)), ((), ())), preferred_element_type=F32
            )
            sums[h, b] = (
                full[:64, :128] + full[64:, 128:],
                full[64:, :128] - full[:64, 128:],
            )
    rows = 64 // holders
    for h in range(2):
        here, there = sums[h, 0], sums[1 - h, 1]
        for ri, value in enumerate((here[0] + there[0], here[1] - there[1])):
            for p in range(holders):
                lay_ref[p, h, ri * rows : (ri + 1) * rows, :] = value[p * rows : (p + 1) * rows]
    out_ref[:, 0] = lay_ref[...].astype(BF16)


def final_call(weighted, cond):
    sources, _, pairs, _, points, _ = weighted.shape
    holders = cond.shape[1]
    rows = 2 * 64 // holders
    return pl.pallas_call(
        final_body,
        out_shape=jax.ShapeDtypeStruct((holders, pairs, 2, rows, 128), BF16),
        grid=(pairs,),
        in_specs=[
            pl.BlockSpec((sources, 2, 1, 2, points, 128), lambda i: (0, 0, i, 0, 0, 0)),
            pl.BlockSpec(
                (2, holders, 1, 2, cond.shape[4], 128), lambda i: (0, 0, i, 0, 0, 0)
            ),
        ],
        out_specs=pl.BlockSpec((holders, 1, 2, rows, 128), lambda i: (0, i, 0, 0, 0)),
        scratch_shapes=[pltpu.VMEM((holders, 2, rows, 128), F32)],
        compiler_params=pltpu.CompilerParams(vmem_limit_bytes=40 * MIB),
    )(weighted, cond)


def swap_mom(value):
    return lax.ppermute(value, "mom", [(0, 1), (1, 0)])


def swap_pts(value, mask):
    return lax.ppermute(value, "pts", [(i, i ^ mask) for i in range(lax.axis_size("pts"))])


def other_val(part):
    middle = part.shape[1] // 2
    here = swap_mom(part)
    by_y = swap_pts(here, 2)
    by_z = swap_pts(here, 4)
    across = [swap_pts(by_z[:, :middle], 2), swap_pts(by_y[:, middle:], 4)]
    groups = [[here], [by_y], [by_z], across]
    return groups + [[swap_pts(piece, 1) for piece in group] for group in groups]


def fast_path(
    amplitudes,
    val_orbitals,
    cond_orbitals,
    screened,
    val_energy,
    cond_energy,
    grid_of_slot,
    opposite_slot,
):
    groups, holders = lax.axis_size("mom"), lax.axis_size("pts")
    mom, pts = lax.axis_index("mom"), lax.axis_index("pts")
    slots = opposite_slot.shape[0]
    total = grid_of_slot.shape[0]
    rows_here = val_energy.shape[1]
    devices = groups * holders
    pairs = slots // devices
    points = screened.shape[2]
    width = val_orbitals.shape[3] // CHUNKS
    eighth = slots // 8

    q = pts % 8
    mine = lax.dynamic_slice_in_dim(val_orbitals, q * eighth, eighth, 1)
    pieces = [other_val(mine[..., c * width : (c + 1) * width]) for c in range(CHUNKS)]

    where = (jnp.arange(groups, dtype=jnp.int32) - mom) % groups
    halves = half_call(amplitudes, cond_orbitals, where, groups)
    half_other = swap_mom(halves[1])

    order = q ^ jnp.array([0, 2, 4, 6, 1, 3, 5, 7], dtype=jnp.int32)
    slot_own = mom * slots + jnp.arange(slots, dtype=jnp.int32)
    slot_other = (1 - mom) * slots + (
        order[:, None] * eighth + jnp.arange(eighth, dtype=jnp.int32)
    ).reshape(slots)
    slot_here = jnp.concatenate([slot_own, slot_other])
    every = jnp.arange(total, dtype=jnp.int32)
    is_opposite = grid_of_slot[None, :] == total - 1 - grid_of_slot[:, None]
    opposite = jnp.sum(jnp.where(is_opposite, every[None, :], 0), axis=1)
    low = jnp.where(every < slots, every, opposite)
    place = low // pairs * (2 * pairs) + low % pairs + jnp.where(every < slots, 0, pairs)
    chosen = slot_here[:, None] == every[None, :]
    grid_here = jnp.sum(jnp.where(chosen, grid_of_slot[None, :], 0), axis=1)
    place_here = jnp.sum(jnp.where(chosen, place[None, :], 0), axis=1)
    phases = every[:, None] * grid_here[None, :] % total
    angles = phases.astype(F32) * (2.0 * math.pi / total)
    cosine = jnp.cos(angles).astype(BF16)
    sine = jnp.sin(angles).astype(BF16)
    forward = jnp.concatenate(
        [jnp.concatenate([cosine, sine], 1), jnp.concatenate([-sine, cosine], 1)], 0
    )
    backward = forward.T * (1.0 / total)

    paired = jnp.where(
        mom == 0, jnp.arange(slots, dtype=jnp.int32), opposite[:slots] - slots
    )
    cond_send = jnp.take(jnp.swapaxes(cond_orbitals, 0, 1), paired, axis=0)
    cond_send = cond_send.reshape((devices, pairs) + cond_send.shape[1:])
    cond_pairs = lax.all_to_all(cond_send, ("mom", "pts"), 0, 0, tiled=True)
    cond_pairs = cond_pairs.reshape((groups, holders) + cond_pairs.shape[1:])

    screen = jnp.transpose(screened, (2, 0, 1, 3))
    summed = None
    for c in range(CHUNKS):
        summed = main_call(
            halves[0],
            half_other,
            val_orbitals,
            c,
            pieces[c],
            screen,
            (forward, backward),
            order * eighth,
            place_here,
            summed,
            c == CHUNKS - 1,
        )
    send = summed.reshape((devices, 2, pairs) + summed.shape[1:])
    weighted = lax.all_to_all(send, ("mom", "pts"), 0, 0, tiled=True)
    combined = final_call(weighted, cond_pairs)
    combined = jnp.concatenate([combined, combined], axis=0)
    back = lax.all_to_all(combined, ("mom", "pts"), 0, 0, tiled=True)

    back = back.reshape(slots, 2, 2, rows_here, -1)
    partner = jnp.where(
        mom == 0, jnp.arange(slots, dtype=jnp.int32), opposite_slot % slots
    )
    back = jnp.take(back, partner, axis=0).astype(F32)
    here = jnp.where(mom == 0, back[:, 0], back[:, 1])
    there = jnp.where(mom == 0, back[:, 1], back[:, 0])
    own_rows = lax.dynamic_slice_in_dim(amplitudes, pts * rows_here, rows_here, 4).astype(F32)
    gap = cond_energy[:, None, :] - val_energy[:, :, None]
    result_real = gap * own_rows[0, 0] - here[:, 0]
    result_imag = gap * own_rows[1, 0] - here[:, 1]
    anti_real = -gap * own_rows[0, 1] + there[:, 0]
    anti_imag = -gap * own_rows[1, 1] - there[:, 1]
    return jnp.stack([jnp.stack([result_real, anti_real]), jnp.stack([result_imag, anti_imag])])


CHUNKS = 2


def fits(mesh, amplitudes, val_orbitals):
    groups, holders = mesh.shape["mom"], mesh.shape["pts"]
    slots = amplitudes.shape[3] // groups
    points = val_orbitals.shape[3] // (groups * holders)
    return (
        groups == 2
        and holders % 8 == 0
        and holders & (holders - 1) == 0
        and slots % (groups * holders) == 0
        and slots % 128 == 0
        and points % 16 == 0
        and amplitudes.shape[2] == 1
        and amplitudes.shape[4:] == (64, 128)
        and val_orbitals.shape[3] % (128 * CHUNKS) == 0
    )


def solution(mesh):
    in_specs = (
        P(None, None, None, "mom", None, None),
        P(None, "mom", None, None),
        P(None, "mom", "pts", None),
        P(None, None, ("pts", "mom"), None),
        P("mom", "pts"),
        P("mom", None),
        P(),
        P("mom"),
    )
    out_specs = P(None, None, None, "mom", "pts", None)

    def apply(*arguments):
        path = fast_path if fits(mesh, *arguments[:2]) else general_path
        return jax.shard_map(
            path, mesh=mesh, in_specs=in_specs, out_specs=out_specs, check_vma=False
        )(*arguments)

    return apply
```

```python
import functools
import math

import jax
import jax.numpy as jnp
from jax import lax
from jax.experimental import pallas as pl
from jax.experimental.pallas import tpu as pltpu
from jax.sharding import PartitionSpec as P


F32 = jnp.float32
BF16 = jnp.bfloat16
MIB = 1024 * 1024


def partner_2(value, axis, apart):
    mask = 2**apart
    pairs = [(source, source ^ mask) for source in range(lax.axis_size(axis))]
    return lax.ppermute(value, axis, pairs)


def complex_mix(formula, left, right, left_sign, right_sign):
    real_real = jnp.einsum(formula, left[0], right[0], preferred_element_type=jnp.float32)
    imag_imag = jnp.einsum(formula, left[1], right[1], preferred_element_type=jnp.float32)
    real_imag = jnp.einsum(formula, left[0], right[1], preferred_element_type=jnp.float32)
    imag_real = jnp.einsum(formula, left[1], right[0], preferred_element_type=jnp.float32)
    return jnp.stack(
        [
            real_real - left_sign * right_sign * imag_imag,
            right_sign * real_imag + left_sign * imag_real,
        ]
    )


def general_path(
    amplitudes,
    val_orbitals,
    cond_orbitals,
    screened,
    val_energy,
    cond_energy,
    grid_of_slot,
    opposite_slot,
):
    slots_here = opposite_slot.shape[0]
    total_slots = grid_of_slot.shape[0]
    rows_here = val_energy.shape[1]
    frequency = jnp.arange(total_slots, dtype=jnp.int32)
    phases = frequency[:, None] * grid_of_slot[None, :] % total_slots
    angles = phases.astype(jnp.float32) * (2.0 * math.pi / total_slots)
    cosine_table = jnp.cos(angles).astype(jnp.bfloat16)
    sine_table = jnp.sin(angles).astype(jnp.bfloat16)
    half_product = complex_mix("bnkvc,kuc->bnkvu", amplitudes, cond_orbitals, 1.0, 1.0).astype(
        jnp.bfloat16
    )
    pair_values = complex_mix("bnkvu,kvm->bnkum", half_product, val_orbitals, 1.0, -1.0).astype(
        jnp.bfloat16
    )
    flattened = pair_values.reshape(pair_values.shape[:4] + (-1,))
    weights = screened.reshape(2, total_slots, -1)
    inverse_count = 1.0 / total_slots
    whole_k = lax.all_to_all(flattened, "mom", split_axis=4, concat_axis=3, tiled=True)
    spec_real = jnp.einsum(
        "fs,bnsc->bnfc", cosine_table, whole_k[0], preferred_element_type=jnp.float32
    ) + jnp.einsum("fs,bnsc->bnfc", sine_table, whole_k[1], preferred_element_type=jnp.float32)
    spec_imag = jnp.einsum(
        "fs,bnsc->bnfc", cosine_table, whole_k[1], preferred_element_type=jnp.float32
    ) - jnp.einsum("fs,bnsc->bnfc", sine_table, whole_k[0], preferred_element_type=jnp.float32)
    prod_real = (weights[0] * spec_real - weights[1] * spec_imag).astype(jnp.bfloat16)
    prod_imag = (weights[0] * spec_imag + weights[1] * spec_real).astype(jnp.bfloat16)
    back_real = (
        jnp.einsum("fs,bnfc->bnsc", cosine_table, prod_real, preferred_element_type=jnp.float32)
        - jnp.einsum("fs,bnfc->bnsc", sine_table, prod_imag, preferred_element_type=jnp.float32)
    ) * inverse_count
    back_imag = (
        jnp.einsum("fs,bnfc->bnsc", cosine_table, prod_imag, preferred_element_type=jnp.float32)
        + jnp.einsum("fs,bnfc->bnsc", sine_table, prod_real, preferred_element_type=jnp.float32)
    ) * inverse_count
    field_pts = lax.all_to_all(
        jnp.stack([back_real, back_imag]).astype(jnp.bfloat16),
        "mom",
        split_axis=3,
        concat_axis=4,
        tiled=True,
    )
    field_pts = field_pts.reshape(pair_values.shape)
    weighted = complex_mix("bnkum,kvm->bnkvu", field_pts, val_orbitals, 1.0, 1.0).astype(
        jnp.bfloat16
    )
    rows_mine = lax.all_to_all(weighted, "pts", split_axis=4, concat_axis=5, tiled=True)
    band_values = complex_mix(
        "bnkvu,kuc->bnkvc",
        rows_mine,
        lax.all_gather(cond_orbitals, "pts", axis=2, tiled=True),
        1.0,
        -1.0,
    )
    top_bit = lax.axis_size("mom").bit_length() - 2
    partner = partner_2(band_values.astype(jnp.bfloat16), "mom", top_bit).astype(band_values.dtype)
    mirrored = jnp.take(partner, opposite_slot % slots_here, axis=3)
    start_row = lax.axis_index("pts") * rows_here
    own_rows = lax.dynamic_slice_in_dim(amplitudes, start_row, rows_here, 4).astype(jnp.float32)
    energy_gap = cond_energy[:, None, :] - val_energy[:, :, None]
    result_real = energy_gap * own_rows[0, 0] - band_values[0, 0] - mirrored[0, 1]
    result_imag = energy_gap * own_rows[1, 0] - band_values[1, 0] + mirrored[1, 1]
    anti_real = -energy_gap * own_rows[0, 1] + band_values[0, 1] + mirrored[0, 0]
    anti_imag = -energy_gap * own_rows[1, 1] + band_values[1, 1] - mirrored[1, 0]
    return jnp.stack([jnp.stack([result_real, anti_real]), jnp.stack([result_imag, anti_imag])])


def half_signs(low, high):
    lane = lax.broadcasted_iota(jnp.int32, (1, 128), 1)
    return jnp.where(lane < 64, low, high).astype(F32)


def half_body(where_ref, amp_ref, cond_ref, out_ref):
    groups, block, _, points, _ = out_ref.shape
    total = groups * points
    signs = half_signs(-1.0, 1.0)
    for kk in range(block):
        cond = cond_ref[:, kk].reshape(2 * total, cond_ref.shape[-1])
        for b in range(2):
            amp = amp_ref[:, b, 0, kk].reshape(128, amp_ref.shape[-1])
            full = lax.dot_general(
                cond, amp, (((1,), (1,)), ((), ())), preferred_element_type=F32
            )
            half = full[:total] + pltpu.roll(full[total:], 64, 1) * signs
            half = half.astype(BF16).reshape(groups, points, 128)
            for g in range(groups):
                out_ref[where_ref[g], kk, b] = half[g]


def half_call(amplitudes, cond_orbitals, where, groups):
    slots, bands = amplitudes.shape[3], amplitudes.shape[5]
    rows = amplitudes.shape[4]
    points = cond_orbitals.shape[2] // groups
    block = 16
    return pl.pallas_call(
        half_body,
        out_shape=jax.ShapeDtypeStruct((groups, slots, 2, points, 128), BF16),
        grid_spec=pltpu.PrefetchScalarGridSpec(
            num_scalar_prefetch=1,
            grid=(slots // block,),
            in_specs=[
                pl.BlockSpec((2, 2, 1, block, rows, bands), lambda i, *_: (0, 0, 0, i, 0, 0)),
                pl.BlockSpec((2, block, groups * points, bands), lambda i, *_: (0, i, 0, 0)),
            ],
            out_specs=pl.BlockSpec(
                (groups, block, 2, points, 128), lambda i, *_: (0, i, 0, 0, 0)
            ),
        ),
        compiler_params=pltpu.CompilerParams(vmem_limit_bytes=40 * MIB),
    )(where, amplitudes, cond_orbitals)


def main_body(layout, base_ref, pos_ref, *refs):
    own_blocks, block, sizes, points, first, last = layout
    half_own, half_other, own_ref = refs[:3]
    count = sum(len(group) for group in sizes)
    flat = list(refs[3 : 3 + count])
    groups = []
    for group in sizes:
        groups.append([flat.pop(0) for _ in group])
    rest = list(refs[3 + count :])
    screen_ref, forward_ref, backward_ref = rest[:3]
    rest = rest[3:]
    before_ref = None if first else rest.pop(0)
    out_ref, pair_ref = rest
    blocks = own_blocks + len(groups)
    total = blocks * block
    rows = 4 * points
    pitch = rows + 1
    lanes = pair_ref.shape[0]
    width = lanes * 128
    step = pl.program_id(0)
    into = half_signs(1.0, -1.0)
    back = half_signs(-1.0, 1.0)

    def make_pairs(source, half_ref, half_start, start, size):
        for kk in range(size):
            half = half_ref[half_start + kk].reshape(2 * points, 128)
            turned = (pltpu.roll(half.astype(F32), 64, 1) * into).astype(BF16)
            stacked = jnp.concatenate([half, turned], axis=0)
            val = source[:, kk].reshape(128, width)
            pairs = jnp.dot(stacked, val, preferred_element_type=F32)
            at = (start + kk) * pitch
            for l in range(lanes):
                pair_ref[l, pl.ds(at, rows), :] = pairs[:, l * 128 : (l + 1) * 128]

    def make_weighted(source, half_ref, half_start, start, size):
        for kk in range(size):
            k = start + kk
            at = k * pitch
            field = jnp.concatenate(
                [pair_ref[l, pl.ds(at, rows), :] for l in range(lanes)], axis=1
            ).astype(BF16)
            val = source[:, kk].reshape(128, width)
            both = lax.dot_general(
                field, val, (((1,), (1,)), ((), ())), preferred_element_type=F32
            )
            half = rows // 2
            weighted = both[:half] + pltpu.roll(both[half:], 64, 1) * back
            if not first:
                weighted = before_ref[k] + weighted
            if last:
                out_ref[pos_ref[k]] = weighted.astype(BF16).reshape(2, points, 128)
            else:
                out_ref[k] = weighted

    def each_block(work, index):
        @pl.when(index < own_blocks)
        def _():
            work(own_ref, half_own, index * block, index * block, block)

        for t, (group, extents) in enumerate(zip(groups, sizes)):

            @pl.when(index == own_blocks + t)
            def _():
                done = 0
                for ref, extent in zip(group, extents):
                    start = (own_blocks + t) * block + done
                    work(ref, half_other, base_ref[t] + done, start, extent)
                    done += extent

    @pl.when(step < blocks)
    def _():
        each_block(make_pairs, step)

    @pl.when((step >= blocks) & (step < blocks + points))
    def _():
        nu = step - blocks
        for l in range(lanes):
            columns = []
            for b in range(2):
                parts = []
                for ri in range(2):
                    row = ri * 2 * points + b * points + nu
                    parts.append(pair_ref[l, pl.ds(row, total, stride=pitch), :].astype(BF16))
                columns.append(jnp.concatenate(parts, axis=0))
            spectrum = jnp.dot(
                forward_ref[...], jnp.concatenate(columns, axis=1), preferred_element_type=F32
            )
            real = screen_ref[0, 0, :, l * 128 : (l + 1) * 128].astype(F32)
            imag = screen_ref[0, 1, :, l * 128 : (l + 1) * 128].astype(F32)
            real = jnp.concatenate([real, real], axis=1)
            imag = jnp.concatenate([imag, imag], axis=1)
            spec_real, spec_imag = spectrum[:total], spectrum[total:]
            prod_real = (real * spec_real - imag * spec_imag).astype(BF16)
            prod_imag = (real * spec_imag + imag * spec_real).astype(BF16)
            field = jnp.dot(
                backward_ref[...],
                jnp.concatenate([prod_real, prod_imag], axis=0),
                preferred_element_type=F32,
            )
            for b in range(2):
                for ri in range(2):
                    row = ri * 2 * points + b * points + nu
                    pair_ref[l, pl.ds(row, total, stride=pitch), :] = field[
                        ri * total : (ri + 1) * total, b * 128 : (b + 1) * 128
                    ]

    @pl.when(step >= blocks + points)
    def _():
        each_block(make_weighted, step - blocks - points)


def main_call(half_own, half_other, own, chunk, pieces, screen, tables, base, pos, before, last):
    slots, _, points, _ = half_own.shape
    bands = own.shape[2]
    block = sum(piece.shape[1] for piece in pieces[0])
    width = pieces[0][0].shape[3]
    own_blocks = slots // block
    blocks = own_blocks + len(pieces)
    total = blocks * block
    first = before is None
    sizes = tuple(tuple(piece.shape[1] for piece in group) for group in pieces)
    flat = [piece for group in pieces for piece in group]

    def own_map(s, *_):
        early = jnp.minimum(s, own_blocks - 1)
        late = jnp.clip(s - blocks - points, 0, own_blocks - 1)
        return (0, jnp.where(s < blocks, early, late), 0, chunk)

    def whole(shape):
        return pl.BlockSpec(
            shape, lambda s, *_: (0,) * len(shape), pipeline_mode=pl.Buffered(1)
        )

    in_specs = [
        whole(half_own.shape),
        whole(half_other.shape),
        pl.BlockSpec((2, block, bands, width), own_map),
    ]
    in_specs += [whole(piece.shape) for piece in flat]
    in_specs += [
        pl.BlockSpec(
            (1, 2, total, width), lambda s, *_: (jnp.clip(s - blocks, 0, points - 1), 0, 0, chunk)
        ),
        whole(tables[0].shape),
        whole(tables[1].shape),
    ]
    operands = [half_own, half_other, own, *flat, screen, *tables]
    if not first:
        in_specs.append(whole(before.shape))
        operands.append(before)
    if last:
        out = jax.ShapeDtypeStruct((total, 2, points, 128), BF16)
    else:
        out = jax.ShapeDtypeStruct((total, 2 * points, 128), F32)
    columns = 2 * points * width
    work = 8 * columns * total * total * 2 + 4 * columns * total * 2 * bands * 4
    traffic = 2 * total * (2 * bands * width * 3 + points * (2 * width + 4 * bands))
    return pl.pallas_call(
        functools.partial(main_body, (own_blocks, block, sizes, points, first, last)),
        out_shape=out,
        grid_spec=pltpu.PrefetchScalarGridSpec(
            num_scalar_prefetch=2,
            grid=(2 * blocks + points,),
            in_specs=in_specs,
            out_specs=whole(out.shape),
            scratch_shapes=[pltpu.VMEM((width // 128, total * (4 * points + 1), 128), F32)],
        ),
        compiler_params=pltpu.CompilerParams(vmem_limit_bytes=62 * MIB),
        cost_estimate=pl.CostEstimate(
            flops=work, bytes_accessed=traffic, transcendentals=0
        ),
    )(base, pos, *operands)


def final_body(weighted_ref, cond_ref, out_ref, lay_ref):
    sources = weighted_ref.shape[0]
    points = weighted_ref.shape[4]
    holders = cond_ref.shape[1]
    groups = sources // holders
    sums = {}
    for h in range(2):
        columns = []
        for ri in range(2):
            parts = []
            for g in range(groups):
                part = cond_ref[h, :, 0, ri, g * points : (g + 1) * points, :]
                parts.append(part.reshape(holders * points, 128))
            columns.append(jnp.concatenate(parts, axis=0))
        cond = jnp.concatenate(columns, axis=1)
        for b in range(2):
            weighted = weighted_ref[:, h, 0, b].reshape(sources * points, 128)
            full = lax.dot_general(
                weighted, cond, (((0,), (0,)), ((), ())), preferred_element_type=F32
            )
            sums[h, b] = (
                full[:64, :128] + full[64:, 128:],
                full[64:, :128] - full[:64, 128:],
            )
    rows = 64 // holders
    for h in range(2):
        here, there = sums[h, 0], sums[1 - h, 1]
        for ri, value in enumerate((here[0] + there[0], here[1] - there[1])):
            for p in range(holders):
                lay_ref[p, h, ri * rows : (ri + 1) * rows, :] = value[p * rows : (p + 1) * rows]
    out_ref[:, 0] = lay_ref[...].astype(BF16)


def final_call(weighted, cond):
    sources, _, pairs, _, points, _ = weighted.shape
    holders = cond.shape[1]
    rows = 2 * 64 // holders
    return pl.pallas_call(
        final_body,
        out_shape=jax.ShapeDtypeStruct((holders, pairs, 2, rows, 128), BF16),
        grid=(pairs,),
        in_specs=[
            pl.BlockSpec((sources, 2, 1, 2, points, 128), lambda i: (0, 0, i, 0, 0, 0)),
            pl.BlockSpec(
                (2, holders, 1, 2, cond.shape[4], 128), lambda i: (0, 0, i, 0, 0, 0)
            ),
        ],
        out_specs=pl.BlockSpec((holders, 1, 2, rows, 128), lambda i: (0, i, 0, 0, 0)),
        scratch_shapes=[pltpu.VMEM((holders, 2, rows, 128), F32)],
        compiler_params=pltpu.CompilerParams(vmem_limit_bytes=40 * MIB),
    )(weighted, cond)


def swap_mom(value):
    return lax.ppermute(value, "mom", [(0, 1), (1, 0)])


def swap_pts(value, mask):
    return lax.ppermute(value, "pts", [(i, i ^ mask) for i in range(lax.axis_size("pts"))])


def gather_chips(here):
    middle = here.shape[1] // 2
    by_y = swap_pts(here, 2)
    by_z = swap_pts(here, 4)
    across = [swap_pts(by_z[:, :middle], 2), swap_pts(by_y[:, middle:], 4)]
    return [[here], [by_y], [by_z], across]


def with_cores(groups):
    return groups + [[swap_pts(piece, 1) for piece in group] for group in groups]


def fast_path(
    amplitudes,
    val_orbitals,
    cond_orbitals,
    screened,
    val_energy,
    cond_energy,
    grid_of_slot,
    opposite_slot,
):
    groups, holders = lax.axis_size("mom"), lax.axis_size("pts")
    mom, pts = lax.axis_index("mom"), lax.axis_index("pts")
    slots = opposite_slot.shape[0]
    total = grid_of_slot.shape[0]
    rows_here = val_energy.shape[1]
    devices = groups * holders
    pairs = slots // devices
    eighth = slots // 8

    q = pts % 8
    mine = lax.dynamic_slice_in_dim(val_orbitals, q * eighth, eighth, 1)
    size = eighth // STREAMS
    fetched = [swap_mom(mine[:, c * size : (c + 1) * size]) for c in range(STREAMS)]

    where = (jnp.arange(groups, dtype=jnp.int32) - mom) % groups
    halves = half_call(amplitudes, cond_orbitals, where, groups)
    fetched[-1], half_sent = lax.optimization_barrier((fetched[-1], halves[1]))
    half_other = swap_mom(half_sent)
    streams = [gather_chips(here) for here in fetched]

    order = q ^ jnp.array([0, 2, 4, 6, 1, 3, 5, 7], dtype=jnp.int32)
    slot_own = mom * slots + jnp.arange(slots, dtype=jnp.int32)
    slot_other = (1 - mom) * slots + (
        order[:, None] * eighth + jnp.arange(eighth, dtype=jnp.int32)
    ).reshape(slots)
    slot_here = jnp.concatenate([slot_own, slot_other])
    every = jnp.arange(total, dtype=jnp.int32)
    is_opposite = grid_of_slot[None, :] == total - 1 - grid_of_slot[:, None]
    opposite = jnp.sum(jnp.where(is_opposite, every[None, :], 0), axis=1)
    low = jnp.where(every < slots, every, opposite)
    place = low // pairs * (2 * pairs) + low % pairs + jnp.where(every < slots, 0, pairs)
    chosen = slot_here[:, None] == every[None, :]
    grid_here = jnp.sum(jnp.where(chosen, grid_of_slot[None, :], 0), axis=1)
    place_here = jnp.sum(jnp.where(chosen, place[None, :], 0), axis=1)
    phases = every[:, None] * grid_here[None, :] % total
    angles = phases.astype(F32) * (2.0 * math.pi / total)
    cosine = jnp.cos(angles).astype(BF16)
    sine = jnp.sin(angles).astype(BF16)
    forward = jnp.concatenate(
        [jnp.concatenate([cosine, sine], 1), jnp.concatenate([-sine, cosine], 1)], 0
    )
    backward = forward.T * (1.0 / total)
    screen = jnp.transpose(screened, (2, 0, 1, 3))

    streams[-1][1], forward, backward, screen, place_here = lax.optimization_barrier(
        (streams[-1][1], forward, backward, screen, place_here)
    )
    streams = [with_cores(stream) for stream in streams]
    pieces = [sum(groups_of, []) for groups_of in zip(*streams)]

    paired = jnp.where(
        mom == 0, jnp.arange(slots, dtype=jnp.int32), opposite[:slots] - slots
    )
    cond_send = jnp.take(jnp.swapaxes(cond_orbitals, 0, 1), paired, axis=0)
    cond_send = cond_send.reshape((devices, pairs) + cond_send.shape[1:])
    cond_send, pieces, half_other = lax.optimization_barrier(
        (cond_send, pieces, half_other)
    )
    cond_pairs = lax.all_to_all(cond_send, ("mom", "pts"), 0, 0, tiled=True)
    cond_pairs = cond_pairs.reshape((groups, holders) + cond_pairs.shape[1:])

    weighted = main_call(
        halves[0],
        half_other,
        val_orbitals,
        0,
        pieces,
        screen,
        (forward, backward),
        order * eighth,
        place_here,
        None,
        True,
    )
    send = weighted.reshape((devices, 2, pairs) + weighted.shape[1:])
    weighted = lax.all_to_all(send, ("mom", "pts"), 0, 0, tiled=True)
    combined = final_call(weighted, cond_pairs)
    combined = jnp.concatenate([combined, combined], axis=0)
    back = lax.all_to_all(combined, ("mom", "pts"), 0, 0, tiled=True)

    back = back.reshape(slots, 2, 2, rows_here, -1)
    partner = jnp.where(
        mom == 0, jnp.arange(slots, dtype=jnp.int32), opposite_slot % slots
    )
    back = jnp.take(back, partner, axis=0).astype(F32)
    here = jnp.where(mom == 0, back[:, 0], back[:, 1])
    there = jnp.where(mom == 0, back[:, 1], back[:, 0])
    own_rows = lax.dynamic_slice_in_dim(amplitudes, pts * rows_here, rows_here, 4).astype(F32)
    gap = cond_energy[:, None, :] - val_energy[:, :, None]
    result_real = gap * own_rows[0, 0] - here[:, 0]
    result_imag = gap * own_rows[1, 0] - here[:, 1]
    anti_real = -gap * own_rows[0, 1] + there[:, 0]
    anti_imag = -gap * own_rows[1, 1] - there[:, 1]
    return jnp.stack([jnp.stack([result_real, anti_real]), jnp.stack([result_imag, anti_imag])])


STREAMS = 2


def fits(mesh, amplitudes, val_orbitals):
    groups, holders = mesh.shape["mom"], mesh.shape["pts"]
    slots = amplitudes.shape[3] // groups
    points = val_orbitals.shape[3] // (groups * holders)
    return (
        groups == 2
        and holders % 8 == 0
        and holders & (holders - 1) == 0
        and slots % (groups * holders) == 0
        and slots % 128 == 0
        and points % 16 == 0
        and amplitudes.shape[2] == 1
        and amplitudes.shape[4:] == (64, 128)
        and slots // 8 % (2 * STREAMS) == 0
        and val_orbitals.shape[3] % 128 == 0
    )


def solution(mesh):
    in_specs = (
        P(None, None, None, "mom", None, None),
        P(None, "mom", None, None),
        P(None, "mom", "pts", None),
        P(None, None, ("pts", "mom"), None),
        P("mom", "pts"),
        P("mom", None),
        P(),
        P("mom"),
    )
    out_specs = P(None, None, None, "mom", "pts", None)

    def apply(*arguments):
        path = fast_path if fits(mesh, *arguments[:2]) else general_path
        return jax.shard_map(
            path, mesh=mesh, in_specs=in_specs, out_specs=out_specs, check_vma=False
        )(*arguments)

    return apply
```

```python
import functools
import math

import jax
import jax.numpy as jnp
from jax import lax
from jax.experimental import pallas as pl
from jax.experimental.pallas import tpu as pltpu
from jax.sharding import PartitionSpec as P


F32 = jnp.float32
BF16 = jnp.bfloat16
MIB = 1024 * 1024


def partner_2(value, axis, apart):
    mask = 2**apart
    pairs = [(source, source ^ mask) for source in range(lax.axis_size(axis))]
    return lax.ppermute(value, axis, pairs)


def complex_mix(formula, left, right, left_sign, right_sign):
    real_real = jnp.einsum(formula, left[0], right[0], preferred_element_type=jnp.float32)
    imag_imag = jnp.einsum(formula, left[1], right[1], preferred_element_type=jnp.float32)
    real_imag = jnp.einsum(formula, left[0], right[1], preferred_element_type=jnp.float32)
    imag_real = jnp.einsum(formula, left[1], right[0], preferred_element_type=jnp.float32)
    return jnp.stack(
        [
            real_real - left_sign * right_sign * imag_imag,
            right_sign * real_imag + left_sign * imag_real,
        ]
    )


def general_path(
    amplitudes,
    val_orbitals,
    cond_orbitals,
    screened,
    val_energy,
    cond_energy,
    grid_of_slot,
    opposite_slot,
):
    slots_here = opposite_slot.shape[0]
    total_slots = grid_of_slot.shape[0]
    rows_here = val_energy.shape[1]
    frequency = jnp.arange(total_slots, dtype=jnp.int32)
    phases = frequency[:, None] * grid_of_slot[None, :] % total_slots
    angles = phases.astype(jnp.float32) * (2.0 * math.pi / total_slots)
    cosine_table = jnp.cos(angles).astype(jnp.bfloat16)
    sine_table = jnp.sin(angles).astype(jnp.bfloat16)
    half_product = complex_mix("bnkvc,kuc->bnkvu", amplitudes, cond_orbitals, 1.0, 1.0).astype(
        jnp.bfloat16
    )
    pair_values = complex_mix("bnkvu,kvm->bnkum", half_product, val_orbitals, 1.0, -1.0).astype(
        jnp.bfloat16
    )
    flattened = pair_values.reshape(pair_values.shape[:4] + (-1,))
    weights = screened.reshape(2, total_slots, -1)
    inverse_count = 1.0 / total_slots
    whole_k = lax.all_to_all(flattened, "mom", split_axis=4, concat_axis=3, tiled=True)
    spec_real = jnp.einsum(
        "fs,bnsc->bnfc", cosine_table, whole_k[0], preferred_element_type=jnp.float32
    ) + jnp.einsum("fs,bnsc->bnfc", sine_table, whole_k[1], preferred_element_type=jnp.float32)
    spec_imag = jnp.einsum(
        "fs,bnsc->bnfc", cosine_table, whole_k[1], preferred_element_type=jnp.float32
    ) - jnp.einsum("fs,bnsc->bnfc", sine_table, whole_k[0], preferred_element_type=jnp.float32)
    prod_real = (weights[0] * spec_real - weights[1] * spec_imag).astype(jnp.bfloat16)
    prod_imag = (weights[0] * spec_imag + weights[1] * spec_real).astype(jnp.bfloat16)
    back_real = (
        jnp.einsum("fs,bnfc->bnsc", cosine_table, prod_real, preferred_element_type=jnp.float32)
        - jnp.einsum("fs,bnfc->bnsc", sine_table, prod_imag, preferred_element_type=jnp.float32)
    ) * inverse_count
    back_imag = (
        jnp.einsum("fs,bnfc->bnsc", cosine_table, prod_imag, preferred_element_type=jnp.float32)
        + jnp.einsum("fs,bnfc->bnsc", sine_table, prod_real, preferred_element_type=jnp.float32)
    ) * inverse_count
    field_pts = lax.all_to_all(
        jnp.stack([back_real, back_imag]).astype(jnp.bfloat16),
        "mom",
        split_axis=3,
        concat_axis=4,
        tiled=True,
    )
    field_pts = field_pts.reshape(pair_values.shape)
    weighted = complex_mix("bnkum,kvm->bnkvu", field_pts, val_orbitals, 1.0, 1.0).astype(
        jnp.bfloat16
    )
    rows_mine = lax.all_to_all(weighted, "pts", split_axis=4, concat_axis=5, tiled=True)
    band_values = complex_mix(
        "bnkvu,kuc->bnkvc",
        rows_mine,
        lax.all_gather(cond_orbitals, "pts", axis=2, tiled=True),
        1.0,
        -1.0,
    )
    top_bit = lax.axis_size("mom").bit_length() - 2
    partner = partner_2(band_values.astype(jnp.bfloat16), "mom", top_bit).astype(band_values.dtype)
    mirrored = jnp.take(partner, opposite_slot % slots_here, axis=3)
    start_row = lax.axis_index("pts") * rows_here
    own_rows = lax.dynamic_slice_in_dim(amplitudes, start_row, rows_here, 4).astype(jnp.float32)
    energy_gap = cond_energy[:, None, :] - val_energy[:, :, None]
    result_real = energy_gap * own_rows[0, 0] - band_values[0, 0] - mirrored[0, 1]
    result_imag = energy_gap * own_rows[1, 0] - band_values[1, 0] + mirrored[1, 1]
    anti_real = -energy_gap * own_rows[0, 1] + band_values[0, 1] + mirrored[0, 0]
    anti_imag = -energy_gap * own_rows[1, 1] + band_values[1, 1] - mirrored[1, 0]
    return jnp.stack([jnp.stack([result_real, anti_real]), jnp.stack([result_imag, anti_imag])])


def half_signs(low, high):
    lane = lax.broadcasted_iota(jnp.int32, (1, 128), 1)
    return jnp.where(lane < 64, low, high).astype(F32)


def half_body(where_ref, amp_ref, cond_ref, out_ref):
    groups, block, _, points, _ = out_ref.shape
    total = groups * points
    signs = half_signs(-1.0, 1.0)
    for kk in range(block):
        cond = cond_ref[:, kk].reshape(2 * total, cond_ref.shape[-1])
        for b in range(2):
            amp = amp_ref[:, b, 0, kk].reshape(128, amp_ref.shape[-1])
            full = lax.dot_general(
                cond, amp, (((1,), (1,)), ((), ())), preferred_element_type=F32
            )
            half = full[:total] + pltpu.roll(full[total:], 64, 1) * signs
            half = half.astype(BF16).reshape(groups, points, 128)
            for g in range(groups):
                out_ref[where_ref[g], kk, b] = half[g]


def half_call(amplitudes, cond_orbitals, where, groups):
    slots, bands = amplitudes.shape[3], amplitudes.shape[5]
    rows = amplitudes.shape[4]
    points = cond_orbitals.shape[2] // groups
    block = 16
    return pl.pallas_call(
        half_body,
        out_shape=jax.ShapeDtypeStruct((groups, slots, 2, points, 128), BF16),
        grid_spec=pltpu.PrefetchScalarGridSpec(
            num_scalar_prefetch=1,
            grid=(slots // block,),
            in_specs=[
                pl.BlockSpec((2, 2, 1, block, rows, bands), lambda i, *_: (0, 0, 0, i, 0, 0)),
                pl.BlockSpec((2, block, groups * points, bands), lambda i, *_: (0, i, 0, 0)),
            ],
            out_specs=pl.BlockSpec(
                (groups, block, 2, points, 128), lambda i, *_: (0, i, 0, 0, 0)
            ),
        ),
        compiler_params=pltpu.CompilerParams(vmem_limit_bytes=40 * MIB),
    )(where, amplitudes, cond_orbitals)


def main_body(layout, base_ref, pos_ref, *refs):
    own_blocks, block, sizes, points, first, last = layout
    half_own, half_other, own_ref = refs[:3]
    count = sum(len(group) for group in sizes)
    flat = list(refs[3 : 3 + count])
    groups = []
    for group in sizes:
        groups.append([flat.pop(0) for _ in group])
    rest = list(refs[3 + count :])
    screen_ref, forward_ref, backward_ref = rest[:3]
    rest = rest[3:]
    before_ref = None if first else rest.pop(0)
    out_ref, pair_ref = rest
    blocks = own_blocks + len(groups)
    total = blocks * block
    rows = 4 * points
    pitch = rows + 1
    lanes = pair_ref.shape[0]
    width = lanes * 128
    step = pl.program_id(0)
    into = half_signs(1.0, -1.0)
    back = half_signs(-1.0, 1.0)

    def make_pairs(source, half_ref, half_start, start, size):
        for kk in range(size):
            half = half_ref[half_start + kk].reshape(2 * points, 128)
            turned = (pltpu.roll(half.astype(F32), 64, 1) * into).astype(BF16)
            stacked = jnp.concatenate([half, turned], axis=0)
            val = source[:, kk].reshape(128, width)
            pairs = jnp.dot(stacked, val, preferred_element_type=F32)
            at = (start + kk) * pitch
            for l in range(lanes):
                pair_ref[l, pl.ds(at, rows), :] = pairs[:, l * 128 : (l + 1) * 128]

    def make_weighted(source, half_ref, half_start, start, size):
        for kk in range(size):
            k = start + kk
            at = k * pitch
            field = jnp.concatenate(
                [pair_ref[l, pl.ds(at, rows), :] for l in range(lanes)], axis=1
            ).astype(BF16)
            val = source[:, kk].reshape(128, width)
            both = lax.dot_general(
                field, val, (((1,), (1,)), ((), ())), preferred_element_type=F32
            )
            half = rows // 2
            weighted = both[:half] + pltpu.roll(both[half:], 64, 1) * back
            if not first:
                weighted = before_ref[k] + weighted
            if last:
                out_ref[pos_ref[k]] = weighted.astype(BF16).reshape(2, points, 128)
            else:
                out_ref[k] = weighted

    def each_block(work, index):
        @pl.when(index < own_blocks)
        def _():
            work(own_ref, half_own, index * block, index * block, block)

        for t, (group, extents) in enumerate(zip(groups, sizes)):

            @pl.when(index == own_blocks + t)
            def _():
                done = 0
                for ref, extent in zip(group, extents):
                    start = (own_blocks + t) * block + done
                    work(ref, half_other, base_ref[t] + done, start, extent)
                    done += extent

    @pl.when(step < blocks)
    def _():
        each_block(make_pairs, step)

    @pl.when((step >= blocks) & (step < blocks + points))
    def _():
        nu = step - blocks
        for l in range(lanes):
            columns = []
            for b in range(2):
                parts = []
                for ri in range(2):
                    row = ri * 2 * points + b * points + nu
                    parts.append(pair_ref[l, pl.ds(row, total, stride=pitch), :].astype(BF16))
                columns.append(jnp.concatenate(parts, axis=0))
            spectrum = jnp.dot(
                forward_ref[...], jnp.concatenate(columns, axis=1), preferred_element_type=F32
            )
            real = screen_ref[0, 0, :, l * 128 : (l + 1) * 128].astype(F32)
            imag = screen_ref[0, 1, :, l * 128 : (l + 1) * 128].astype(F32)
            real = jnp.concatenate([real, real], axis=1)
            imag = jnp.concatenate([imag, imag], axis=1)
            spec_real, spec_imag = spectrum[:total], spectrum[total:]
            prod_real = (real * spec_real - imag * spec_imag).astype(BF16)
            prod_imag = (real * spec_imag + imag * spec_real).astype(BF16)
            field = jnp.dot(
                backward_ref[...],
                jnp.concatenate([prod_real, prod_imag], axis=0),
                preferred_element_type=F32,
            )
            for b in range(2):
                for ri in range(2):
                    row = ri * 2 * points + b * points + nu
                    pair_ref[l, pl.ds(row, total, stride=pitch), :] = field[
                        ri * total : (ri + 1) * total, b * 128 : (b + 1) * 128
                    ]

    @pl.when(step >= blocks + points)
    def _():
        each_block(make_weighted, step - blocks - points)


def main_call(half_own, half_other, own, chunk, pieces, screen, tables, base, pos, before, last):
    slots, _, points, _ = half_own.shape
    bands = own.shape[2]
    block = sum(piece.shape[1] for piece in pieces[0])
    width = pieces[0][0].shape[3]
    own_blocks = slots // block
    blocks = own_blocks + len(pieces)
    total = blocks * block
    first = before is None
    sizes = tuple(tuple(piece.shape[1] for piece in group) for group in pieces)
    flat = [piece for group in pieces for piece in group]

    def own_map(s, *_):
        early = jnp.minimum(s, own_blocks - 1)
        late = jnp.clip(s - blocks - points, 0, own_blocks - 1)
        return (0, jnp.where(s < blocks, early, late), 0, chunk)

    def whole(shape):
        return pl.BlockSpec(
            shape, lambda s, *_: (0,) * len(shape), pipeline_mode=pl.Buffered(1)
        )

    in_specs = [
        whole(half_own.shape),
        whole(half_other.shape),
        pl.BlockSpec((2, block, bands, width), own_map),
    ]
    in_specs += [whole(piece.shape) for piece in flat]
    in_specs += [
        pl.BlockSpec(
            (1, 2, total, width), lambda s, *_: (jnp.clip(s - blocks, 0, points - 1), 0, 0, chunk)
        ),
        whole(tables[0].shape),
        whole(tables[1].shape),
    ]
    operands = [half_own, half_other, own, *flat, screen, *tables]
    if not first:
        in_specs.append(whole(before.shape))
        operands.append(before)
    if last:
        out = jax.ShapeDtypeStruct((total, 2, points, 128), BF16)
    else:
        out = jax.ShapeDtypeStruct((total, 2 * points, 128), F32)
    columns = 2 * points * width
    work = 8 * columns * total * total * 2 + 4 * columns * total * 2 * bands * 4
    traffic = 2 * total * (2 * bands * width * 3 + points * (2 * width + 4 * bands))
    return pl.pallas_call(
        functools.partial(main_body, (own_blocks, block, sizes, points, first, last)),
        out_shape=out,
        grid_spec=pltpu.PrefetchScalarGridSpec(
            num_scalar_prefetch=2,
            grid=(2 * blocks + points,),
            in_specs=in_specs,
            out_specs=whole(out.shape),
            scratch_shapes=[pltpu.VMEM((width // 128, total * (4 * points + 1), 128), F32)],
        ),
        compiler_params=pltpu.CompilerParams(vmem_limit_bytes=62 * MIB),
        cost_estimate=pl.CostEstimate(
            flops=work, bytes_accessed=traffic, transcendentals=0
        ),
    )(base, pos, *operands)


def final_body(weighted_ref, cond_ref, out_ref, lay_ref):
    sources = weighted_ref.shape[0]
    points = weighted_ref.shape[4]
    holders = cond_ref.shape[1]
    groups = sources // holders
    sums = {}
    for h in range(2):
        columns = []
        for ri in range(2):
            parts = []
            for g in range(groups):
                part = cond_ref[h, :, 0, ri, g * points : (g + 1) * points, :]
                parts.append(part.reshape(holders * points, 128))
            columns.append(jnp.concatenate(parts, axis=0))
        cond = jnp.concatenate(columns, axis=1)
        for b in range(2):
            weighted = weighted_ref[:, h, 0, b].reshape(sources * points, 128)
            full = lax.dot_general(
                weighted, cond, (((0,), (0,)), ((), ())), preferred_element_type=F32
            )
            sums[h, b] = (
                full[:64, :128] + full[64:, 128:],
                full[64:, :128] - full[:64, 128:],
            )
    rows = 64 // holders
    for h in range(2):
        here, there = sums[h, 0], sums[1 - h, 1]
        for ri, value in enumerate((here[0] + there[0], here[1] - there[1])):
            for p in range(holders):
                lay_ref[p, h, ri * rows : (ri + 1) * rows, :] = value[p * rows : (p + 1) * rows]
    out_ref[:, 0] = lay_ref[...].astype(BF16)


def final_call(weighted, cond):
    sources, _, pairs, _, points, _ = weighted.shape
    holders = cond.shape[1]
    rows = 2 * 64 // holders
    return pl.pallas_call(
        final_body,
        out_shape=jax.ShapeDtypeStruct((holders, pairs, 2, rows, 128), BF16),
        grid=(pairs,),
        in_specs=[
            pl.BlockSpec((sources, 2, 1, 2, points, 128), lambda i: (0, 0, i, 0, 0, 0)),
            pl.BlockSpec(
                (2, holders, 1, 2, cond.shape[4], 128), lambda i: (0, 0, i, 0, 0, 0)
            ),
        ],
        out_specs=pl.BlockSpec((holders, 1, 2, rows, 128), lambda i: (0, i, 0, 0, 0)),
        scratch_shapes=[pltpu.VMEM((holders, 2, rows, 128), F32)],
        compiler_params=pltpu.CompilerParams(vmem_limit_bytes=40 * MIB),
    )(weighted, cond)


def swap_mom(value):
    return lax.ppermute(value, "mom", [(0, 1), (1, 0)])


def swap_pts(value, mask):
    return lax.ppermute(value, "pts", [(i, i ^ mask) for i in range(lax.axis_size("pts"))])


def gather_chips(here):
    middle = here.shape[1] // 2
    by_y = swap_pts(here, 2)
    by_z = swap_pts(here, 4)
    across = [swap_pts(by_z[:, :middle], 2), swap_pts(by_y[:, middle:], 4)]
    return [[here], [by_y], [by_z], across]


def with_cores(groups):
    return groups + [[swap_pts(piece, 1) for piece in group] for group in groups]


def fast_path(
    amplitudes,
    val_orbitals,
    cond_orbitals,
    screened,
    val_energy,
    cond_energy,
    grid_of_slot,
    opposite_slot,
):
    groups, holders = lax.axis_size("mom"), lax.axis_size("pts")
    mom, pts = lax.axis_index("mom"), lax.axis_index("pts")
    slots = opposite_slot.shape[0]
    total = grid_of_slot.shape[0]
    rows_here = val_energy.shape[1]
    devices = groups * holders
    pairs = slots // devices
    eighth = slots // 8

    q = pts % 8
    mine = lax.dynamic_slice_in_dim(val_orbitals, q * eighth, eighth, 1)
    size = eighth // STREAMS
    fetched = [swap_mom(mine[:, c * size : (c + 1) * size]) for c in range(STREAMS)]

    where = (jnp.arange(groups, dtype=jnp.int32) - mom) % groups
    halves = half_call(amplitudes, cond_orbitals, where, groups)
    screen = jnp.transpose(screened, (2, 0, 1, 3))
    fetched[-1], half_sent, screen = lax.optimization_barrier(
        (fetched[-1], halves[1], screen)
    )
    streams = [with_cores(gather_chips(here)) for here in fetched]
    pieces = [sum(groups_of, []) for groups_of in zip(*streams)]

    order = q ^ jnp.array([0, 2, 4, 6, 1, 3, 5, 7], dtype=jnp.int32)
    slot_own = mom * slots + jnp.arange(slots, dtype=jnp.int32)
    slot_other = (1 - mom) * slots + (
        order[:, None] * eighth + jnp.arange(eighth, dtype=jnp.int32)
    ).reshape(slots)
    slot_here = jnp.concatenate([slot_own, slot_other])
    every = jnp.arange(total, dtype=jnp.int32)
    is_opposite = grid_of_slot[None, :] == total - 1 - grid_of_slot[:, None]
    opposite = jnp.sum(jnp.where(is_opposite, every[None, :], 0), axis=1)
    low = jnp.where(every < slots, every, opposite)
    place = low // pairs * (2 * pairs) + low % pairs + jnp.where(every < slots, 0, pairs)
    chosen = slot_here[:, None] == every[None, :]
    grid_here = jnp.sum(jnp.where(chosen, grid_of_slot[None, :], 0), axis=1)
    place_here = jnp.sum(jnp.where(chosen, place[None, :], 0), axis=1)
    phases = every[:, None] * grid_here[None, :] % total
    angles = phases.astype(F32) * (2.0 * math.pi / total)
    cosine = jnp.cos(angles).astype(BF16)
    sine = jnp.sin(angles).astype(BF16)
    forward = jnp.concatenate(
        [jnp.concatenate([cosine, sine], 1), jnp.concatenate([-sine, cosine], 1)], 0
    )
    turned = grid_here[:, None] * every[None, :] % total
    turned = turned.astype(F32) * (2.0 * math.pi / total)
    cosine = jnp.cos(turned).astype(BF16) * (1.0 / total)
    sine = jnp.sin(turned).astype(BF16) * (1.0 / total)
    backward = jnp.concatenate(
        [jnp.concatenate([cosine, -sine], 1), jnp.concatenate([sine, cosine], 1)], 0
    )

    paired = jnp.where(
        mom == 0, jnp.arange(slots, dtype=jnp.int32), opposite[:slots] - slots
    )
    cond_send = jnp.take(jnp.swapaxes(cond_orbitals, 0, 1), paired, axis=0, mode="clip")
    cond_send = cond_send.reshape((devices, pairs) + cond_send.shape[1:])
    half_sent, forward, backward, place_here, cond_send = lax.optimization_barrier(
        (half_sent, forward, backward, place_here, cond_send)
    )
    half_other = swap_mom(half_sent)
    cond_send, pieces, half_other = lax.optimization_barrier(
        (cond_send, pieces, half_other)
    )
    cond_pairs = lax.all_to_all(cond_send, ("mom", "pts"), 0, 0, tiled=True)
    cond_pairs = cond_pairs.reshape((groups, holders) + cond_pairs.shape[1:])

    weighted = main_call(
        halves[0],
        half_other,
        val_orbitals,
        0,
        pieces,
        screen,
        (forward, backward),
        order * eighth,
        place_here,
        None,
        True,
    )
    send = weighted.reshape((devices, 2, pairs) + weighted.shape[1:])
    weighted = lax.all_to_all(send, ("mom", "pts"), 0, 0, tiled=True)
    combined = final_call(weighted, cond_pairs)
    combined = jnp.concatenate([combined, combined], axis=0)
    back = lax.all_to_all(combined, ("mom", "pts"), 0, 0, tiled=True)

    back = back.reshape(slots, 2, 2, rows_here, -1)
    partner = jnp.where(
        mom == 0, jnp.arange(slots, dtype=jnp.int32), opposite_slot % slots
    )
    back = jnp.take(back, partner, axis=0, mode="clip").astype(F32)
    here = jnp.where(mom == 0, back[:, 0], back[:, 1])
    there = jnp.where(mom == 0, back[:, 1], back[:, 0])
    own_rows = lax.dynamic_slice_in_dim(amplitudes, pts * rows_here, rows_here, 4).astype(F32)
    gap = cond_energy[:, None, :] - val_energy[:, :, None]
    result_real = gap * own_rows[0, 0] - here[:, 0]
    result_imag = gap * own_rows[1, 0] - here[:, 1]
    anti_real = -gap * own_rows[0, 1] + there[:, 0]
    anti_imag = -gap * own_rows[1, 1] - there[:, 1]
    return jnp.stack([jnp.stack([result_real, anti_real]), jnp.stack([result_imag, anti_imag])])


STREAMS = 2


def fits(mesh, amplitudes, val_orbitals):
    groups, holders = mesh.shape["mom"], mesh.shape["pts"]
    slots = amplitudes.shape[3] // groups
    points = val_orbitals.shape[3] // (groups * holders)
    return (
        groups == 2
        and holders % 8 == 0
        and holders & (holders - 1) == 0
        and slots % (groups * holders) == 0
        and slots % 128 == 0
        and points % 16 == 0
        and amplitudes.shape[2] == 1
        and amplitudes.shape[4:] == (64, 128)
        and slots // 8 % (2 * STREAMS) == 0
        and val_orbitals.shape[3] % 128 == 0
    )


def solution(mesh):
    in_specs = (
        P(None, None, None, "mom", None, None),
        P(None, "mom", None, None),
        P(None, "mom", "pts", None),
        P(None, None, ("pts", "mom"), None),
        P("mom", "pts"),
        P("mom", None),
        P(),
        P("mom"),
    )
    out_specs = P(None, None, None, "mom", "pts", None)

    def apply(*arguments):
        path = fast_path if fits(mesh, *arguments[:2]) else general_path
        return jax.shard_map(
            path, mesh=mesh, in_specs=in_specs, out_specs=out_specs, check_vma=False
        )(*arguments)

    return apply
```

```python
import functools
import math

import jax
import jax.numpy as jnp
from jax import lax
from jax.experimental import pallas as pl
from jax.experimental.pallas import tpu as pltpu
from jax.sharding import PartitionSpec as P


F32 = jnp.float32
BF16 = jnp.bfloat16
MIB = 1024 * 1024


def partner_2(value, axis, apart):
    mask = 2**apart
    pairs = [(source, source ^ mask) for source in range(lax.axis_size(axis))]
    return lax.ppermute(value, axis, pairs)


def complex_mix(formula, left, right, left_sign, right_sign):
    real_real = jnp.einsum(formula, left[0], right[0], preferred_element_type=jnp.float32)
    imag_imag = jnp.einsum(formula, left[1], right[1], preferred_element_type=jnp.float32)
    real_imag = jnp.einsum(formula, left[0], right[1], preferred_element_type=jnp.float32)
    imag_real = jnp.einsum(formula, left[1], right[0], preferred_element_type=jnp.float32)
    return jnp.stack(
        [
            real_real - left_sign * right_sign * imag_imag,
            right_sign * real_imag + left_sign * imag_real,
        ]
    )


def general_path(
    amplitudes,
    val_orbitals,
    cond_orbitals,
    screened,
    val_energy,
    cond_energy,
    grid_of_slot,
    opposite_slot,
):
    slots_here = opposite_slot.shape[0]
    total_slots = grid_of_slot.shape[0]
    rows_here = val_energy.shape[1]
    frequency = jnp.arange(total_slots, dtype=jnp.int32)
    phases = frequency[:, None] * grid_of_slot[None, :] % total_slots
    angles = phases.astype(jnp.float32) * (2.0 * math.pi / total_slots)
    cosine_table = jnp.cos(angles).astype(jnp.bfloat16)
    sine_table = jnp.sin(angles).astype(jnp.bfloat16)
    half_product = complex_mix("bnkvc,kuc->bnkvu", amplitudes, cond_orbitals, 1.0, 1.0).astype(
        jnp.bfloat16
    )
    pair_values = complex_mix("bnkvu,kvm->bnkum", half_product, val_orbitals, 1.0, -1.0).astype(
        jnp.bfloat16
    )
    flattened = pair_values.reshape(pair_values.shape[:4] + (-1,))
    weights = screened.reshape(2, total_slots, -1)
    inverse_count = 1.0 / total_slots
    whole_k = lax.all_to_all(flattened, "mom", split_axis=4, concat_axis=3, tiled=True)
    spec_real = jnp.einsum(
        "fs,bnsc->bnfc", cosine_table, whole_k[0], preferred_element_type=jnp.float32
    ) + jnp.einsum("fs,bnsc->bnfc", sine_table, whole_k[1], preferred_element_type=jnp.float32)
    spec_imag = jnp.einsum(
        "fs,bnsc->bnfc", cosine_table, whole_k[1], preferred_element_type=jnp.float32
    ) - jnp.einsum("fs,bnsc->bnfc", sine_table, whole_k[0], preferred_element_type=jnp.float32)
    prod_real = (weights[0] * spec_real - weights[1] * spec_imag).astype(jnp.bfloat16)
    prod_imag = (weights[0] * spec_imag + weights[1] * spec_real).astype(jnp.bfloat16)
    back_real = (
        jnp.einsum("fs,bnfc->bnsc", cosine_table, prod_real, preferred_element_type=jnp.float32)
        - jnp.einsum("fs,bnfc->bnsc", sine_table, prod_imag, preferred_element_type=jnp.float32)
    ) * inverse_count
    back_imag = (
        jnp.einsum("fs,bnfc->bnsc", cosine_table, prod_imag, preferred_element_type=jnp.float32)
        + jnp.einsum("fs,bnfc->bnsc", sine_table, prod_real, preferred_element_type=jnp.float32)
    ) * inverse_count
    field_pts = lax.all_to_all(
        jnp.stack([back_real, back_imag]).astype(jnp.bfloat16),
        "mom",
        split_axis=3,
        concat_axis=4,
        tiled=True,
    )
    field_pts = field_pts.reshape(pair_values.shape)
    weighted = complex_mix("bnkum,kvm->bnkvu", field_pts, val_orbitals, 1.0, 1.0).astype(
        jnp.bfloat16
    )
    rows_mine = lax.all_to_all(weighted, "pts", split_axis=4, concat_axis=5, tiled=True)
    band_values = complex_mix(
        "bnkvu,kuc->bnkvc",
        rows_mine,
        lax.all_gather(cond_orbitals, "pts", axis=2, tiled=True),
        1.0,
        -1.0,
    )
    top_bit = lax.axis_size("mom").bit_length() - 2
    partner = partner_2(band_values.astype(jnp.bfloat16), "mom", top_bit).astype(band_values.dtype)
    mirrored = jnp.take(partner, opposite_slot % slots_here, axis=3)
    start_row = lax.axis_index("pts") * rows_here
    own_rows = lax.dynamic_slice_in_dim(amplitudes, start_row, rows_here, 4).astype(jnp.float32)
    energy_gap = cond_energy[:, None, :] - val_energy[:, :, None]
    result_real = energy_gap * own_rows[0, 0] - band_values[0, 0] - mirrored[0, 1]
    result_imag = energy_gap * own_rows[1, 0] - band_values[1, 0] + mirrored[1, 1]
    anti_real = -energy_gap * own_rows[0, 1] + band_values[0, 1] + mirrored[0, 0]
    anti_imag = -energy_gap * own_rows[1, 1] + band_values[1, 1] - mirrored[1, 0]
    return jnp.stack([jnp.stack([result_real, anti_real]), jnp.stack([result_imag, anti_imag])])


def half_signs(low, high):
    lane = lax.broadcasted_iota(jnp.int32, (1, 128), 1)
    return jnp.where(lane < 64, low, high).astype(F32)


def half_body(where_ref, amp_ref, cond_ref, out_ref):
    groups, block, _, points, _ = out_ref.shape
    total = groups * points
    signs = half_signs(-1.0, 1.0)
    for kk in range(block):
        cond = cond_ref[:, kk].reshape(2 * total, cond_ref.shape[-1])
        for b in range(2):
            amp = amp_ref[:, b, 0, kk].reshape(128, amp_ref.shape[-1])
            full = lax.dot_general(
                cond, amp, (((1,), (1,)), ((), ())), preferred_element_type=F32
            )
            half = full[:total] + pltpu.roll(full[total:], 64, 1) * signs
            half = half.astype(BF16).reshape(groups, points, 128)
            for g in range(groups):
                out_ref[where_ref[g], kk, b] = half[g]


def half_call(amplitudes, cond_orbitals, where, groups):
    slots, bands = amplitudes.shape[3], amplitudes.shape[5]
    rows = amplitudes.shape[4]
    points = cond_orbitals.shape[2] // groups
    block = 16
    return pl.pallas_call(
        half_body,
        out_shape=jax.ShapeDtypeStruct((groups, slots, 2, points, 128), BF16),
        grid_spec=pltpu.PrefetchScalarGridSpec(
            num_scalar_prefetch=1,
            grid=(slots // block,),
            in_specs=[
                pl.BlockSpec((2, 2, 1, block, rows, bands), lambda i, *_: (0, 0, 0, i, 0, 0)),
                pl.BlockSpec((2, block, groups * points, bands), lambda i, *_: (0, i, 0, 0)),
            ],
            out_specs=pl.BlockSpec(
                (groups, block, 2, points, 128), lambda i, *_: (0, i, 0, 0, 0)
            ),
        ),
        compiler_params=pltpu.CompilerParams(vmem_limit_bytes=40 * MIB),
    )(where, amplitudes, cond_orbitals)


def main_body(layout, base_ref, pos_ref, *refs):
    own_blocks, block, sizes, points = layout
    half_own, half_other, own_ref = refs[:3]
    count = sum(len(group) for group in sizes)
    pieces = refs[3 : 3 + count]
    screen_ref, forward_ref, backward_ref, out_ref, pair_ref, held_ref, sems = refs[3 + count :]
    blocks = own_blocks + len(sizes)
    total = blocks * block
    rows = 4 * points
    pitch = rows + 1
    lanes = pair_ref.shape[0]
    width = lanes * 128
    step = pl.program_id(0)
    into = half_signs(1.0, -1.0)
    back = half_signs(-1.0, 1.0)

    def make_pairs(source, half_ref, half_start, start, offset):
        for kk in range(block):
            half = half_ref[half_start + kk].reshape(2 * points, 128)
            turned = (pltpu.roll(half.astype(F32), 64, 1) * into).astype(BF16)
            stacked = jnp.concatenate([half, turned], axis=0)
            val = source[:, offset + kk].reshape(128, width)
            pairs = jnp.dot(stacked, val, preferred_element_type=F32)
            at = (start + kk) * pitch
            for l in range(lanes):
                pair_ref[l, pl.ds(at, rows), :] = pairs[:, l * 128 : (l + 1) * 128]

    def make_weighted(source, half_ref, half_start, start, offset):
        for kk in range(block):
            k = start + kk
            at = k * pitch
            field = jnp.concatenate(
                [pair_ref[l, pl.ds(at, rows), :] for l in range(lanes)], axis=1
            ).astype(BF16)
            val = source[:, offset + kk].reshape(128, width)
            both = lax.dot_general(
                field, val, (((1,), (1,)), ((), ())), preferred_element_type=F32
            )
            half = rows // 2
            weighted = both[:half] + pltpu.roll(both[half:], 64, 1) * back
            out_ref[pos_ref[k]] = weighted.astype(BF16).reshape(2, points, 128)

    def each_block(work, index):
        @pl.when(index < own_blocks)
        def _():
            work(own_ref, half_own, index * block, index * block, 0)

        @pl.when(index >= own_blocks)
        def _():
            t = index - own_blocks
            work(held_ref, half_other, base_ref[t], index * block, t * block)

    copies = []
    number = 0
    for t, extents in enumerate(sizes):
        start = t * block
        copies.append([])
        for extent in extents:
            copies[-1].append(
                pltpu.make_async_copy(
                    pieces[number], held_ref.at[:, pl.ds(start, extent)], sems.at[number]
                )
            )
            start += extent
            number += 1

    for t, group in enumerate(copies):

        @pl.when(step == min(t, own_blocks - 1))
        def _():
            for copy in group:
                copy.start()

    for t, group in enumerate(copies):

        @pl.when(step == own_blocks + t)
        def _():
            for copy in group:
                copy.wait()

    @pl.when(step < blocks)
    def _():
        each_block(make_pairs, step)

    @pl.when((step >= blocks) & (step < blocks + points))
    def _():
        nu = step - blocks
        for l in range(lanes):
            columns = []
            for b in range(2):
                parts = []
                for ri in range(2):
                    row = ri * 2 * points + b * points + nu
                    parts.append(pair_ref[l, pl.ds(row, total, stride=pitch), :].astype(BF16))
                columns.append(jnp.concatenate(parts, axis=0))
            spectrum = jnp.dot(
                forward_ref[...], jnp.concatenate(columns, axis=1), preferred_element_type=F32
            )
            real = screen_ref[0, 0, :, l * 128 : (l + 1) * 128].astype(F32)
            imag = screen_ref[0, 1, :, l * 128 : (l + 1) * 128].astype(F32)
            real = jnp.concatenate([real, real], axis=1)
            imag = jnp.concatenate([imag, imag], axis=1)
            spec_real, spec_imag = spectrum[:total], spectrum[total:]
            prod_real = (real * spec_real - imag * spec_imag).astype(BF16)
            prod_imag = (real * spec_imag + imag * spec_real).astype(BF16)
            field = jnp.dot(
                backward_ref[...],
                jnp.concatenate([prod_real, prod_imag], axis=0),
                preferred_element_type=F32,
            )
            for b in range(2):
                for ri in range(2):
                    row = ri * 2 * points + b * points + nu
                    pair_ref[l, pl.ds(row, total, stride=pitch), :] = field[
                        ri * total : (ri + 1) * total, b * 128 : (b + 1) * 128
                    ]

    @pl.when(step >= blocks + points)
    def _():
        each_block(make_weighted, step - blocks - points)


def main_call(half_own, half_other, own, pieces, screen, tables, base, pos):
    slots, _, points, _ = half_own.shape
    bands = own.shape[2]
    block = sum(piece.shape[1] for piece in pieces[0])
    width = pieces[0][0].shape[3]
    own_blocks = slots // block
    blocks = own_blocks + len(pieces)
    total = blocks * block
    sizes = tuple(tuple(piece.shape[1] for piece in group) for group in pieces)
    flat = [piece for group in pieces for piece in group]

    def own_map(s, *_):
        early = jnp.minimum(s, own_blocks - 1)
        late = jnp.clip(s - blocks - points, 0, own_blocks - 1)
        return (0, jnp.where(s < blocks, early, late), 0, 0)

    def whole(shape):
        return pl.BlockSpec(
            shape, lambda s, *_: (0,) * len(shape), pipeline_mode=pl.Buffered(1)
        )

    in_specs = [
        whole(half_own.shape),
        whole(half_other.shape),
        pl.BlockSpec((2, block, bands, width), own_map),
    ]
    in_specs += [pl.BlockSpec(memory_space=pl.ANY) for _ in flat]
    in_specs += [
        pl.BlockSpec(
            (1, 2, total, width), lambda s, *_: (jnp.clip(s - blocks, 0, points - 1), 0, 0, 0)
        ),
        whole(tables[0].shape),
        whole(tables[1].shape),
    ]
    operands = [half_own, half_other, own, *flat, screen, *tables]
    out = jax.ShapeDtypeStruct((total, 2, points, 128), BF16)
    columns = 2 * points * width
    work = 8 * columns * total * total * 2 + 4 * columns * total * 2 * bands * 4
    traffic = 2 * total * (2 * bands * width * 3 + points * (2 * width + 4 * bands))
    return pl.pallas_call(
        functools.partial(main_body, (own_blocks, block, sizes, points)),
        out_shape=out,
        grid_spec=pltpu.PrefetchScalarGridSpec(
            num_scalar_prefetch=2,
            grid=(2 * blocks + points,),
            in_specs=in_specs,
            out_specs=whole(out.shape),
            scratch_shapes=[
                pltpu.VMEM((width // 128, total * (4 * points + 1), 128), F32),
                pltpu.VMEM((2, len(pieces) * block, bands, width), BF16),
                pltpu.SemaphoreType.DMA((len(flat),)),
            ],
        ),
        compiler_params=pltpu.CompilerParams(vmem_limit_bytes=62 * MIB),
        cost_estimate=pl.CostEstimate(
            flops=work, bytes_accessed=traffic, transcendentals=0
        ),
    )(base, pos, *operands)


def final_body(weighted_ref, cond_ref, out_ref, lay_ref):
    sources = weighted_ref.shape[0]
    points = weighted_ref.shape[4]
    holders = cond_ref.shape[1]
    groups = sources // holders
    sums = {}
    for h in range(2):
        columns = []
        for ri in range(2):
            parts = []
            for g in range(groups):
                part = cond_ref[h, :, 0, ri, g * points : (g + 1) * points, :]
                parts.append(part.reshape(holders * points, 128))
            columns.append(jnp.concatenate(parts, axis=0))
        cond = jnp.concatenate(columns, axis=1)
        for b in range(2):
            weighted = weighted_ref[:, h, 0, b].reshape(sources * points, 128)
            full = lax.dot_general(
                weighted, cond, (((0,), (0,)), ((), ())), preferred_element_type=F32
            )
            sums[h, b] = (
                full[:64, :128] + full[64:, 128:],
                full[64:, :128] - full[:64, 128:],
            )
    rows = 64 // holders
    for h in range(2):
        here, there = sums[h, 0], sums[1 - h, 1]
        for ri, value in enumerate((here[0] + there[0], here[1] - there[1])):
            for p in range(holders):
                lay_ref[p, h, ri * rows : (ri + 1) * rows, :] = value[p * rows : (p + 1) * rows]
    out_ref[:, 0] = lay_ref[...].astype(BF16)


def final_call(weighted, cond):
    sources, _, pairs, _, points, _ = weighted.shape
    holders = cond.shape[1]
    rows = 2 * 64 // holders
    return pl.pallas_call(
        final_body,
        out_shape=jax.ShapeDtypeStruct((holders, pairs, 2, rows, 128), BF16),
        grid=(pairs,),
        in_specs=[
            pl.BlockSpec((sources, 2, 1, 2, points, 128), lambda i: (0, 0, i, 0, 0, 0)),
            pl.BlockSpec(
                (2, holders, 1, 2, cond.shape[4], 128), lambda i: (0, 0, i, 0, 0, 0)
            ),
        ],
        out_specs=pl.BlockSpec((holders, 1, 2, rows, 128), lambda i: (0, i, 0, 0, 0)),
        scratch_shapes=[pltpu.VMEM((holders, 2, rows, 128), F32)],
        compiler_params=pltpu.CompilerParams(vmem_limit_bytes=40 * MIB),
    )(weighted, cond)


def swap_mom(value):
    return lax.ppermute(value, "mom", [(0, 1), (1, 0)])


def swap_pts(value, mask):
    return lax.ppermute(value, "pts", [(i, i ^ mask) for i in range(lax.axis_size("pts"))])


def gather_chips(here):
    middle = here.shape[1] // 2
    by_y = swap_pts(here, 2)
    by_z = swap_pts(here, 4)
    across = [swap_pts(by_z[:, :middle], 2), swap_pts(by_y[:, middle:], 4)]
    return [[here], [by_y], [by_z], across]


def with_cores(groups):
    return groups + [[swap_pts(piece, 1) for piece in group] for group in groups]


def fast_path(
    amplitudes,
    val_orbitals,
    cond_orbitals,
    screened,
    val_energy,
    cond_energy,
    grid_of_slot,
    opposite_slot,
):
    groups, holders = lax.axis_size("mom"), lax.axis_size("pts")
    mom, pts = lax.axis_index("mom"), lax.axis_index("pts")
    slots = opposite_slot.shape[0]
    total = grid_of_slot.shape[0]
    rows_here = val_energy.shape[1]
    devices = groups * holders
    pairs = slots // devices
    eighth = slots // 8

    q = pts % 8
    mine = lax.dynamic_slice_in_dim(val_orbitals, q * eighth, eighth, 1)
    size = eighth // STREAMS
    fetched = [swap_mom(mine[:, c * size : (c + 1) * size]) for c in range(STREAMS)]

    where = (jnp.arange(groups, dtype=jnp.int32) - mom) % groups
    halves = half_call(amplitudes, cond_orbitals, where, groups)
    screen = jnp.transpose(screened, (2, 0, 1, 3))
    fetched[-1], half_sent = lax.optimization_barrier((fetched[-1], halves[1]))
    streams = [with_cores(gather_chips(here)) for here in fetched]
    pieces = [sum(groups_of, []) for groups_of in zip(*streams)]

    order = q ^ jnp.array([0, 2, 4, 6, 1, 3, 5, 7], dtype=jnp.int32)
    slot_own = mom * slots + jnp.arange(slots, dtype=jnp.int32)
    slot_other = (1 - mom) * slots + (
        order[:, None] * eighth + jnp.arange(eighth, dtype=jnp.int32)
    ).reshape(slots)
    slot_here = jnp.concatenate([slot_own, slot_other])
    every = jnp.arange(total, dtype=jnp.int32)
    is_opposite = grid_of_slot[None, :] == total - 1 - grid_of_slot[:, None]
    opposite = jnp.sum(jnp.where(is_opposite, every[None, :], 0), axis=1)
    low = jnp.where(every < slots, every, opposite)
    place = low // pairs * (2 * pairs) + low % pairs + jnp.where(every < slots, 0, pairs)
    chosen = slot_here[:, None] == every[None, :]
    grid_here = jnp.sum(jnp.where(chosen, grid_of_slot[None, :], 0), axis=1)
    place_here = jnp.sum(jnp.where(chosen, place[None, :], 0), axis=1)
    phases = every[:, None] * grid_here[None, :] % total
    angles = phases.astype(F32) * (2.0 * math.pi / total)
    cosine = jnp.cos(angles).astype(BF16)
    sine = jnp.sin(angles).astype(BF16)
    forward = jnp.concatenate(
        [jnp.concatenate([cosine, sine], 1), jnp.concatenate([-sine, cosine], 1)], 0
    )
    turned = grid_here[:, None] * every[None, :] % total
    turned = turned.astype(F32) * (2.0 * math.pi / total)
    cosine = jnp.cos(turned).astype(BF16) * (1.0 / total)
    sine = jnp.sin(turned).astype(BF16) * (1.0 / total)
    backward = jnp.concatenate(
        [jnp.concatenate([cosine, -sine], 1), jnp.concatenate([sine, cosine], 1)], 0
    )

    paired = jnp.where(
        mom == 0, jnp.arange(slots, dtype=jnp.int32), opposite[:slots] - slots
    )
    cond_send = jnp.take(jnp.swapaxes(cond_orbitals, 0, 1), paired, axis=0, mode="clip")
    cond_send = cond_send.reshape((devices, pairs) + cond_send.shape[1:])
    half_sent, forward, backward, place_here, cond_send, screen = lax.optimization_barrier(
        (half_sent, forward, backward, place_here, cond_send, screen)
    )
    half_other = swap_mom(half_sent)
    cond_send, pieces, half_other = lax.optimization_barrier(
        (cond_send, pieces, half_other)
    )
    cond_pairs = lax.all_to_all(cond_send, ("mom", "pts"), 0, 0, tiled=True)
    cond_pairs = cond_pairs.reshape((groups, holders) + cond_pairs.shape[1:])

    weighted = main_call(
        halves[0],
        half_other,
        val_orbitals,
        pieces,
        screen,
        (forward, backward),
        order * eighth,
        place_here,
    )
    send = weighted.reshape((devices, 2, pairs) + weighted.shape[1:])
    weighted = lax.all_to_all(send, ("mom", "pts"), 0, 0, tiled=True)
    combined = final_call(weighted, cond_pairs)
    combined = jnp.concatenate([combined, combined], axis=0)
    back = lax.all_to_all(combined, ("mom", "pts"), 0, 0, tiled=True)

    back = back.reshape(slots, 2, 2, rows_here, -1)
    partner = jnp.where(
        mom == 0, jnp.arange(slots, dtype=jnp.int32), opposite_slot % slots
    )
    back = jnp.take(back, partner, axis=0, mode="clip").astype(F32)
    here = jnp.where(mom == 0, back[:, 0], back[:, 1])
    there = jnp.where(mom == 0, back[:, 1], back[:, 0])
    own_rows = lax.dynamic_slice_in_dim(amplitudes, pts * rows_here, rows_here, 4).astype(F32)
    gap = cond_energy[:, None, :] - val_energy[:, :, None]
    result_real = gap * own_rows[0, 0] - here[:, 0]
    result_imag = gap * own_rows[1, 0] - here[:, 1]
    anti_real = -gap * own_rows[0, 1] + there[:, 0]
    anti_imag = -gap * own_rows[1, 1] - there[:, 1]
    return jnp.stack([jnp.stack([result_real, anti_real]), jnp.stack([result_imag, anti_imag])])


STREAMS = 2


def fits(mesh, amplitudes, val_orbitals):
    groups, holders = mesh.shape["mom"], mesh.shape["pts"]
    slots = amplitudes.shape[3] // groups
    points = val_orbitals.shape[3] // (groups * holders)
    return (
        groups == 2
        and holders % 8 == 0
        and holders & (holders - 1) == 0
        and slots % (groups * holders) == 0
        and slots % 128 == 0
        and points % 16 == 0
        and amplitudes.shape[2] == 1
        and amplitudes.shape[4:] == (64, 128)
        and slots // 8 % (2 * STREAMS) == 0
        and val_orbitals.shape[3] % 128 == 0
    )


def solution(mesh):
    in_specs = (
        P(None, None, None, "mom", None, None),
        P(None, "mom", None, None),
        P(None, "mom", "pts", None),
        P(None, None, ("pts", "mom"), None),
        P("mom", "pts"),
        P("mom", None),
        P(),
        P("mom"),
    )
    out_specs = P(None, None, None, "mom", "pts", None)

    def apply(*arguments):
        path = fast_path if fits(mesh, *arguments[:2]) else general_path
        return jax.shard_map(
            path, mesh=mesh, in_specs=in_specs, out_specs=out_specs, check_vma=False
        )(*arguments)

    return apply
```
